256 devices in a mesh: expert: 16 (over z, core), latent: 8 (over y, x_lo), row: 2 (over x_hi).
Axes of the slice: x: 4 (x_hi: 2, x_lo: 2; x = x_hi * 2 + x_lo), y: 4, z: 8, core: 2. Of those that a mesh axis runs over, the one named last changes fastest.
Arguments:
- model_acts: bfloat16 [512, 8192], P('row', 'expert'), may hold values from -6 to 6
- enc_weight: bfloat16 [8192, 12288], P('expert', ('latent', 'row')), may hold values from -0.0625 to 0.0625
- dec_weight: bfloat16 [12288, 8192], P(('latent', 'row'), 'expert'), may hold values from -0.0546875 to 0.0546875
- enc_bias: float32 [12288], P('latent'), may hold values from -3 to 3
- dec_bias: float32 [8192], P('expert'), may hold values from -3 to 3
- enc_first: bfloat16 [8192, 12288], P('expert', ('latent', 'row')), may hold values from -0.119628906 to 0.119628906
- enc_second: bfloat16 [8192, 12288], P('expert', ('latent', 'row')), may hold values from 9.9658966e-05 to 0.0099487305
- dec_first: bfloat16 [12288, 8192], P(('latent', 'row'), 'expert'), may hold values from -0.119628906 to 0.119628906
- dec_second: bfloat16 [12288, 8192], P(('latent', 'row'), 'expert'), may hold values from 9.9658966e-05 to 0.0099487305
Outputs:
- encoder_next: bfloat16 [8192, 12288], P('expert', ('latent', 'row'))
- decoder_next: bfloat16 [12288, 8192], P(('latent', 'row'), 'expert')
- enc_first_next: bfloat16 [8192, 12288], P('expert', ('latent', 'row'))
- enc_second_next: bfloat16 [8192, 12288], P('expert', ('latent', 'row'))
- dec_first_next: bfloat16 [12288, 8192], P(('latent', 'row'), 'expert')
- dec_second_next: bfloat16 [12288, 8192], P(('latent', 'row'), 'expert')
- enc_bias_grad: float32 [12288], P(('latent', 'row'))
- dec_bias_grad: float32 [8192], P('expert')
The draws below stay inside these ranges and needn't reach their ends.
All inputs are finite; a program needn't handle non-finite values.
Results may differ from the reference program's by a relative error of at most 0.005.
Values may be sent and summed in bfloat16 or wider, within the bound.
A program may use at most 64 MiB of HBM per device.

```python
import math
import jax
import jax.numpy as jnp
from jax import lax

EXPERTS = 8
D = 1024
L = 12288
ROWS = 512


def steps_of(own_key, extent, split, least, high):
    gain = 1.0
    for dim, blocks in split:
        draws = jax.random.uniform(jax.random.fold_in(jax.random.fold_in(own_key, 6), dim), (blocks,), jnp.float32, least / len(split), high / len(split))
        gain = gain * jnp.repeat(jnp.exp(draws), extent[dim] // blocks).reshape((-1,) + (1,) * (len(extent) - 1 - dim))
    return gain


def bell_draw(own_key, shape, deviation, reach, shards=(), held_as=jnp.bfloat16):
    entries = jax.random.normal(own_key, shape, jnp.float32) * deviation
    if len(shards) > 0:
        entries = steps_of(own_key, shape, shards, -0.22, 0.18) * entries
    return jnp.clip(entries, min=-reach, max=reach).astype(held_as)


def setup_inputs(seed: int = 0) -> dict:
    splits = jax.random.split(jax.random.key(seed), 10)
    model_acts = bell_draw(splits[0], (ROWS, EXPERTS * D), 1.0, 6.0, ((0, 2), (1, 16)))
    enc_weight = bell_draw(splits[1], (EXPERTS * D, L), (EXPERTS * D) ** -0.5, 0.0625, ((0, 16), (1, 16)))
    dec_weight = bell_draw(splits[2], (L, EXPERTS * D), L ** -0.5, 0.0546875, ((0, 16), (1, 16)))
    enc_bias = bell_draw(splits[3], (L,), 0.5, 3.0, ((0, 8),), jnp.float32)
    dec_bias = bell_draw(splits[4], (EXPERTS * D,), 0.5, 3.0, ((0, 16),), jnp.float32)
    enc_first = bell_draw(splits[5], (EXPERTS * D, L), 0.02, 0.119628906, ((0, 16), (1, 16)))
    enc_second = jnp.clip(jnp.exp(math.log(0.0099487305) - 4.603446 * jax.random.uniform(splits[6], (EXPERTS * D, L), jnp.float32) ** steps_of(splits[6], (EXPERTS * D, L), ((0, 16), (1, 16)), -0.2, 0.2)), 9.965896606445312e-05, 0.0099487305).astype(jnp.bfloat16)
    dec_first = bell_draw(splits[7], (L, EXPERTS * D), 0.02, 0.119628906, ((0, 16), (1, 16)))
    dec_second = jnp.clip(jnp.exp(math.log(0.0099487305) - 4.603446 * jax.random.uniform(splits[8], (L, EXPERTS * D), jnp.float32) ** steps_of(splits[8], (L, EXPERTS * D), ((0, 16), (1, 16)), -0.2, 0.2)), 9.965896606445312e-05, 0.0099487305).astype(jnp.bfloat16)
    return {"model_acts": model_acts, "enc_weight": enc_weight, "dec_weight": dec_weight, "enc_bias": enc_bias, "dec_bias": dec_bias, "enc_first": enc_first, "enc_second": enc_second, "dec_first": dec_first, "dec_second": dec_second}


beta_one = 0.9
beta_two = 0.999
learn_rate = 0.001
adam_eps = 1e-08
bias_one = 0.9999734386011124
bias_two = 0.09520785288629115
norm_eps = 1e-06
sparsity = 1.0

def adam_step(weight, moment_one, moment_two, gradient):
    first_next = beta_one * moment_one.astype(jnp.float32) + (1.0 - beta_one) * gradient
    second_next = beta_two * moment_two.astype(jnp.float32) + (1.0 - beta_two) * gradient * gradient
    stepped = weight.astype(jnp.float32) - learn_rate * (first_next / bias_one) / (jnp.sqrt(second_next / bias_two) + adam_eps)
    return (stepped.astype(jnp.bfloat16), first_next.astype(jnp.bfloat16), second_next.astype(jnp.bfloat16))

def reference(model_acts, enc_weight, dec_weight, enc_bias, dec_bias, enc_first, enc_second, dec_first, dec_second):
    total_rows = model_acts.shape[0]
    preact = jnp.dot(model_acts, enc_weight, preferred_element_type=jnp.float32) + enc_bias
    latent_low = jnp.maximum(preact, 0.0).astype(jnp.bfloat16)
    rebuilt = jnp.dot(latent_low, dec_weight, preferred_element_type=jnp.float32) + dec_bias
    grad_rows = 2.0 * (rebuilt - model_acts.astype(jnp.float32)) / total_rows
    grad_low = grad_rows.astype(jnp.bfloat16)
    decoder_wide = dec_weight.astype(jnp.float32).reshape(L, EXPERTS, D)
    decoder_norms = jnp.sqrt(lax.optimization_barrier(jnp.sum(decoder_wide * decoder_wide, axis=2)) + norm_eps)
    strength = lax.optimization_barrier(jnp.sum(decoder_norms, axis=1))
    col_total = lax.optimization_barrier(jnp.sum(latent_low.astype(jnp.float32), axis=0)) / total_rows
    dec_grad = jnp.dot(latent_low.T, grad_low, preferred_element_type=jnp.float32)
    dec_grad = dec_grad + sparsity * col_total[:, None] * (decoder_wide / decoder_norms[:, :, None]).reshape(L, EXPERTS * D)
    dec_bias_grad = lax.optimization_barrier(jnp.sum(grad_rows, axis=0))
    back_grad = jnp.dot(grad_low, dec_weight.T, preferred_element_type=jnp.float32) + sparsity * strength / total_rows
    grad_pre = jnp.where(preact > 0, back_grad, 0.0).astype(jnp.bfloat16)
    enc_grad = jnp.dot(model_acts.T, grad_pre, preferred_element_type=jnp.float32)
    enc_bias_grad = lax.optimization_barrier(jnp.sum(grad_pre.astype(jnp.float32), axis=0))
    encoder_next, enc_first_next, enc_second_next = adam_step(enc_weight, enc_first, enc_second, enc_grad)
    decoder_next, dec_first_next, dec_second_next = adam_step(dec_weight, dec_first, dec_second, dec_grad)
    return (encoder_next, decoder_next, enc_first_next, enc_second_next, dec_first_next, dec_second_next, enc_bias_grad, dec_bias_grad)
```

```python
import functools

import jax
import jax.numpy as jnp
from jax import lax
from jax.experimental import pallas as pl
from jax.experimental.pallas import tpu as pltpu
from jax.sharding import PartitionSpec as P

beta_one = 0.9
beta_two = 0.999
learn_rate = 0.001
adam_eps = 1e-08
bias_one = 0.9999734386011124
bias_two = 0.09520785288629115
norm_eps = 1e-06
sparsity = 1.0

MESH = pl.DeviceIdType.MESH
F32 = jnp.float32
BF16 = jnp.bfloat16

CHIPS = 8
SIDE = 4
LANES = 128
FAR_Z = (4, 3, 5, 2, 6, 1, 7)
FAR_XY = tuple(
    sorted(
        ((a, b) for a in range(SIDE) for b in range(SIDE) if a or b),
        key=lambda s: -(min(s[0], SIDE - s[0]) + min(s[1], SIDE - s[1])),
    )
)


def dot_nt(left, right):
    return lax.dot_general(
        left, right, (((1,), (1,)), ((), ())), preferred_element_type=F32
    )


def dot_tn(left, right):
    return lax.dot_general(
        left, right, (((0,), (0,)), ((), ())), preferred_element_type=F32
    )


def dot_nn(left, right):
    return jnp.dot(left, right, preferred_element_type=F32)


def adam_step(weight, moment_one, moment_two, gradient):
    first_next = beta_one * moment_one.astype(F32) + (1.0 - beta_one) * gradient
    second_next = (
        beta_two * moment_two.astype(F32) + (1.0 - beta_two) * gradient * gradient
    )
    stepped = weight.astype(F32) - learn_rate * (first_next / bias_one) / (
        jnp.sqrt(second_next / bias_two) + adam_eps
    )
    return stepped.astype(BF16), first_next.astype(BF16), second_next.astype(BF16)


def exchange_kernel(
    acts_hbm, enc_hbm, dec_hbm, m_hbm, v_hbm, ebias_ref, dbias_ref,
    tok_out, gpre_out, w_out, m_out, v_out, rsum_out,
    tok, enc, dec, lat, grad, gpre,
    keep, give_wide, took_wide, give, took, half, rs_wide, rs_z, pre,
    rb, rb_low, rs_xy,
    sq_lane, norm_lane, sq_col, norm_col,
    m_old, v_old, w_new, m_new, v_new,
    load_sem, store_sem, send_sem, recv_sem,
):
    rows, width = acts_hbm.shape
    latents = enc_hbm.shape[1]
    total_rows = 2 * rows
    side = rows // 2
    piece = side // CHIPS
    xy_piece = total_rows // (SIDE * SIDE)
    lines = latents // LANES

    e, l, r = (lax.axis_index(a) for a in ("expert", "latent", "row"))
    z, c = lax.div(e, 2), lax.rem(e, 2)
    y, x = lax.div(l, 2), 2 * r + lax.rem(l, 2)

    def at_z(step):
        return lax.rem(z + step, CHIPS)

    def z_peer(step):
        return (at_z(step) * 2 + c, l, r)

    def at_xy(dx, dy):
        return lax.rem(x + dx, SIDE), lax.rem(y + dy, SIDE)

    def xy_peer(dx, dy):
        px, py = at_xy(dx, dy)
        return (e, py * 2 + lax.rem(px, 2), lax.div(px, 2))

    pair = (z * 2 + 1 - c, l, r)
    mirror_x = SIDE - 1 - x
    mirror = (e, y * 2 + lax.rem(mirror_x, 2), lax.div(mirror_x, 2))

    count = [0]
    sent = []

    def send(src, dst, to):
        n = count[0]
        count[0] += 1
        copy = pltpu.make_async_remote_copy(
            src_ref=src, dst_ref=dst, send_sem=send_sem.at[n], recv_sem=recv_sem.at[n],
            device_id=to, device_id_type=MESH,
        )
        copy.start()
        sent.append(copy)
        return copy

    def arrived(copies):
        for copy in copies:
            copy.wait_recv()

    def span(start, size):
        return pl.ds(pl.multiple_of(start, size), size)

    own_base, other_base = r * rows, (1 - r) * rows
    own_rows = span(own_base, rows)
    my_piece = c * side + z * piece

    loads = [
        pltpu.make_async_copy(src, dst, load_sem.at[n])
        for n, (src, dst) in enumerate(
            (
                (acts_hbm, tok.at[own_rows]), (enc_hbm, enc), (dec_hbm, dec),
                (m_hbm, m_old), (v_hbm, v_old),
            )
        )
    ]
    barrier = pltpu.get_barrier_semaphore()
    greeted = [*(z_peer(s) for s in FAR_Z), *(xy_peer(*s) for s in FAR_XY), pair]
    for to in greeted:
        pl.semaphore_signal(barrier, inc=1, device_id=to, device_id_type=MESH)
    for load in loads:
        load.start()

    def encode_part(k, base):
        give_wide[k] = dot_nn(tok[span(base + (1 - c) * side, side)], enc[...])
        keep[k] = dot_nn(tok[span(base + c * side, side)], enc[...])

    loads[0].wait()
    loads[1].wait()
    encode_part(0, own_base)
    loads[2].wait()
    wide = dec[...].astype(F32)
    square = wide * wide
    high = square.astype(BF16)
    low = (square - high.astype(F32)).astype(BF16)
    ones_lane = jnp.ones((8, width), BF16)
    ones_col = jnp.ones((width, LANES), BF16)
    lane = dot_nt(ones_lane, high) + dot_nt(ones_lane, low)
    sq_lane[0] = jnp.concatenate(
        [lane[0:1, n * LANES : (n + 1) * LANES] for n in range(lines)]
        + [jnp.zeros((8 - lines, LANES), F32)],
        axis=0,
    )
    sq_col[0] = dot_nn(high, ones_col) + dot_nn(low, ones_col)
    pl.semaphore_wait(barrier, len(greeted))

    acts_copy = send(tok.at[own_rows], tok.at[own_rows], mirror)
    core_a = send(give_wide.at[0], took_wide.at[0], pair)
    lane_copy = send(sq_lane.at[0], sq_lane.at[1], pair)

    def z_scatter(values, slots):
        return [
            send(values.at[span(at_z(s) * piece, piece)], slots.at[s], z_peer(s))
            for s in FAR_Z
        ]

    def z_summed(k, copies, slots):
        arrived(copies)
        total = keep[k, span(z * piece, piece)]
        for s in range(1, CHIPS):
            total = total + slots[s].astype(F32)
        return total

    def z_gather(buf, base):
        at = span(base + my_piece, piece)
        return [send(buf.at[at], buf.at[at], z_peer(s)) for s in FAR_Z]

    def z_forward(buf, base, copies):
        arrived(copies)
        at = span(base + c * side, side)
        return send(buf.at[at], buf.at[at], pair)

    core_a.wait_recv()
    keep[0] = keep[0] + took_wide[0]
    scatter_a = z_scatter(keep.at[0], rs_wide.at[0])
    acts_copy.wait_recv()
    encode_part(1, other_base)
    core_b = send(give_wide.at[1], took_wide.at[1], pair)
    col_copy = send(sq_col.at[0], sq_col.at[1], pair)
    core_b.wait_recv()
    keep[1] = keep[1] + took_wide[1]
    scatter_b = z_scatter(keep.at[1], rs_wide.at[1])

    tok_store = pltpu.make_async_copy(tok, tok_out, store_sem.at[0])
    tok_store.start()
    lane_copy.wait_recv()
    norm_lane[0] = jnp.sqrt(sq_lane[0] + sq_lane[1] + norm_eps)
    norm_copies = [send(norm_lane.at[0], norm_lane.at[s], z_peer(s)) for s in FAR_Z]
    bias = jnp.concatenate(
        [ebias_ref[pl.ds(r * lines + n, 1), :] for n in range(lines)], axis=1
    )
    col_copy.wait_recv()
    norm_col[...] = jnp.sqrt(sq_col[0] + sq_col[1] + norm_eps)

    def encode(k, base, index, copies):
        value = z_summed(k, copies, rs_wide.at[k]) + bias
        pre[index] = value
        lat[span(base + my_piece, piece)] = jnp.maximum(value, 0.0).astype(BF16)
        return z_gather(lat, base)

    gather_a = encode(0, own_base, r, scatter_a)
    gather_b = encode(1, other_base, 1 - r, scatter_b)
    forward_a = z_forward(lat, own_base, gather_a)
    forward_b = z_forward(lat, other_base, gather_b)

    def rebuild(base, core):
        at = span(base + core * side, side)
        part = dot_nn(lat[at], dec[...])
        rb[at] = part
        rb_low[at] = part.astype(BF16)

    rebuild(own_base, c)
    rebuild(other_base, c)
    forward_a.wait_recv()
    rebuild(own_base, 1 - c)
    forward_b.wait_recv()
    rebuild(other_base, 1 - c)

    scatter = []
    for dx, dy in FAR_XY:
        px, py = at_xy(dx, dy)
        at = span((px * SIDE + py) * xy_piece, xy_piece)
        scatter.append(send(rb_low.at[at], rs_xy.at[dx * SIDE + dy], xy_peer(dx, dy)))
    dbias = jnp.concatenate(
        [dbias_ref[n : n + 1, :] for n in range(width // LANES)], axis=1
    )
    arrived(scatter)
    mine = span((x * SIDE + y) * xy_piece, xy_piece)
    total = rb[mine]
    for n in range(1, SIDE * SIDE):
        total = total + rs_xy[n].astype(F32)
    grad_rows = 2.0 * (total + dbias - tok[mine].astype(F32)) / total_rows
    grad[mine] = grad_rows.astype(BF16)
    gather = [send(grad.at[mine], grad.at[mine], xy_peer(*s)) for s in FAR_XY]

    arrived(norm_copies)
    strength = norm_lane[0]
    for s in range(1, CHIPS):
        strength = strength + norm_lane[s]
    strength = (sparsity / total_rows) * strength
    penalty = jnp.concatenate([strength[n : n + 1, :] for n in range(lines)], axis=1)
    arrived(gather)

    def back_start(k, base):
        give[k] = dot_nt(grad[span(base + (1 - c) * side, side)], dec[...]).astype(BF16)
        copy = send(give.at[k], took.at[k], pair)
        keep[k + 2] = dot_nt(grad[span(base + c * side, side)], dec[...])
        return copy

    def back_scatter(k, copy):
        copy.wait_recv()
        total = keep[k + 2] + took[k].astype(F32)
        keep[k + 2] = total
        half[k] = total.astype(BF16)
        return z_scatter(half.at[k], rs_z.at[k])

    core_a = back_start(0, 0)
    core_b = back_start(1, rows)
    scatter_a = back_scatter(0, core_a)
    scatter_b = back_scatter(1, core_b)

    loads[3].wait()
    loads[4].wait()
    ones_rows = jnp.ones((total_rows, LANES), BF16)

    def decoder_block(n, carry):
        at = span(n * LANES, LANES)
        acts = lat[:, at]
        gradient = dot_tn(acts, grad[...])
        factor = (sparsity / total_rows) * dot_tn(acts, ones_rows) / norm_col[at]
        weight = dec[at]
        gradient = gradient + jnp.tile(factor, (1, width // LANES)) * weight.astype(F32)
        w_new[at], m_new[at], v_new[at] = adam_step(weight, m_old[at], v_old[at], gradient)
        return carry

    lax.fori_loop(0, lines, decoder_block, 0)
    stores = [
        tok_store,
        pltpu.make_async_copy(w_new, w_out, store_sem.at[1]),
        pltpu.make_async_copy(m_new, m_out, store_sem.at[2]),
        pltpu.make_async_copy(v_new, v_out, store_sem.at[3]),
    ]
    for store in stores[1:]:
        store.start()

    def back(k, base, copies):
        value = z_summed(k + 2, copies, rs_z.at[k]) + penalty
        value = jnp.where(pre[k] > 0, value, 0.0)
        gpre[span(base + my_piece, piece)] = value.astype(BF16)
        return z_gather(gpre, base)

    gather_a = back(0, 0, scatter_a)
    gather_b = back(1, rows, scatter_b)
    row_sum = dot_nn(jnp.ones((8, total_rows), BF16), grad[...])
    rsum_out[...] = jnp.concatenate(
        [row_sum[0:1, n * LANES : (n + 1) * LANES] for n in range(width // LANES)], axis=0
    )
    forward_a = z_forward(gpre, 0, gather_a)
    forward_b = z_forward(gpre, rows, gather_b)
    forward_a.wait_recv()
    forward_b.wait_recv()
    stores.append(pltpu.make_async_copy(gpre, gpre_out, store_sem.at[4]))
    stores[-1].start()
    for copy in sent:
        copy.wait_send()
    for store in stores:
        store.wait()


def exchange(acts, enc_weight, dec_weight, dec_first, dec_second, enc_bias, dec_bias):
    rows, width = acts.shape
    latents = enc_weight.shape[1]
    total_rows = 2 * rows
    side = rows // 2
    piece = side // CHIPS
    xy_piece = total_rows // (SIDE * SIDE)
    sems = 104
    hbm = pl.BlockSpec(memory_space=pltpu.HBM)
    vmem = pl.BlockSpec(memory_space=pltpu.VMEM)
    dec_shape = (latents, width)
    return pl.pallas_call(
        exchange_kernel,
        name="exchange",
        out_shape=(
            jax.ShapeDtypeStruct((total_rows, width), BF16),
            jax.ShapeDtypeStruct((total_rows, latents), BF16),
            jax.ShapeDtypeStruct(dec_shape, BF16),
            jax.ShapeDtypeStruct(dec_shape, BF16),
            jax.ShapeDtypeStruct(dec_shape, BF16),
            jax.ShapeDtypeStruct((width // LANES, LANES), F32),
        ),
        in_specs=[hbm] * 5 + [vmem] * 2,
        out_specs=(hbm,) * 5 + (vmem,),
        scratch_shapes=[
            pltpu.VMEM((total_rows, width), BF16),
            pltpu.VMEM((width, latents), BF16),
            pltpu.VMEM(dec_shape, BF16),
            pltpu.VMEM((total_rows, latents), BF16),
            pltpu.VMEM((total_rows, width), BF16),
            pltpu.VMEM((total_rows, latents), BF16),
            pltpu.VMEM((4, side, latents), F32),
            pltpu.VMEM((2, side, latents), F32),
            pltpu.VMEM((2, side, latents), F32),
            pltpu.VMEM((2, side, latents), BF16),
            pltpu.VMEM((2, side, latents), BF16),
            pltpu.VMEM((2, side, latents), BF16),
            pltpu.VMEM((2, CHIPS, piece, latents), F32),
            pltpu.VMEM((2, CHIPS, piece, latents), BF16),
            pltpu.VMEM((2, piece, latents), F32),
            pltpu.VMEM((total_rows, width), F32),
            pltpu.VMEM((total_rows, width), BF16),
            pltpu.VMEM((SIDE * SIDE, xy_piece, width), BF16),
            pltpu.VMEM((2, 8, LANES), F32),
            pltpu.VMEM((CHIPS, 8, LANES), F32),
            pltpu.VMEM((2, latents, LANES), F32),
            pltpu.VMEM((latents, LANES), F32),
            *[pltpu.VMEM(dec_shape, BF16)] * 5,
            pltpu.SemaphoreType.DMA((5,)),
            pltpu.SemaphoreType.DMA((5,)),
            pltpu.SemaphoreType.DMA((sems,)),
            pltpu.SemaphoreType.DMA((sems,)),
        ],
        compiler_params=pltpu.CompilerParams(
            collective_id=0, has_side_effects=True, vmem_limit_bytes=60 << 20
        ),
    )(acts, enc_weight, dec_weight, dec_first, dec_second, enc_bias, dec_bias)


def finish_kernel(
    tok_ref, gpre_ref, w, m, v, rsum_ref, w_done, m_done, v_done,
    w_next, m_next, v_next, bsum_out, rsum_out, w_out, m_out, v_out,
):
    @pl.when(pl.program_id(0) == 0)
    def _():
        total = dot_nn(jnp.ones((8, gpre_ref.shape[0]), BF16), gpre_ref[...])
        for n in range(bsum_out.shape[0]):
            bsum_out[n : n + 1, :] = total[0:1, n * LANES : (n + 1) * LANES]
        rsum_out[...] = rsum_ref[...]

    gradient = dot_tn(tok_ref[...], gpre_ref[...])
    w_next[...], m_next[...], v_next[...] = adam_step(w[...], m[...], v[...], gradient)
    w_out[...] = w_done[...]
    m_out[...] = m_done[...]
    v_out[...] = v_done[...]


def finish(tok, gpre, w, m, v, row_sum, decoder, blocks=4):
    total_rows, latents = gpre.shape
    width = w.shape[0]
    block = pl.BlockSpec((width // blocks, latents), lambda i: (i, 0))
    turned = pl.BlockSpec((latents // blocks, width), lambda i: (i, 0))

    def whole(shape):
        return pl.BlockSpec(shape, lambda i: (0, 0))

    shapes = (latents // LANES, LANES), (width // LANES, LANES)
    return pl.pallas_call(
        finish_kernel,
        name="finish",
        grid=(blocks,),
        out_shape=(jax.ShapeDtypeStruct(w.shape, BF16),) * 3
        + tuple(jax.ShapeDtypeStruct(s, F32) for s in shapes)
        + (jax.ShapeDtypeStruct(decoder[0].shape, BF16),) * 3,
        in_specs=[
            pl.BlockSpec((total_rows, width // blocks), lambda i: (0, i)),
            whole((total_rows, latents)), block, block, block, whole(shapes[1]),
            turned, turned, turned,
        ],
        out_specs=(block,) * 3 + tuple(whole(s) for s in shapes) + (turned,) * 3,
        compiler_params=pltpu.CompilerParams(vmem_limit_bytes=56 << 20),
    )(tok, gpre, w, m, v, row_sum, *decoder)


def local(
    model_acts, enc_weight, dec_weight, enc_bias, dec_bias,
    enc_first, enc_second, dec_first, dec_second,
):
    tok, gpre, *decoder, row_sum = exchange(
        model_acts, enc_weight, dec_weight, dec_first, dec_second,
        enc_bias.reshape(-1, LANES), dec_bias.reshape(-1, LANES),
    )
    encoder = finish(tok, gpre, enc_weight, enc_first, enc_second, row_sum, decoder)
    enc_next, enc_m, enc_v, bias_sum, row_sum, dec_next, dec_m, dec_v = encoder
    return (
        enc_next, dec_next, enc_m, enc_v, dec_m, dec_v,
        bias_sum.reshape(-1), row_sum.reshape(-1),
    )


def solution(mesh):
    split = P("expert", ("latent", "row"))
    turned = P(("latent", "row"), "expert")
    return jax.shard_map(
        local,
        mesh=mesh,
        in_specs=(
            P("row", "expert"), split, turned, P("latent"), P("expert"),
            split, split, turned, turned,
        ),
        out_specs=(
            split, turned, split, split, turned, turned,
            P(("latent", "row")), P("expert"),
        ),
        check_vma=False,
    )
```

```python
import functools

import jax
import jax.numpy as jnp
from jax import lax
from jax.experimental import pallas as pl
from jax.experimental.pallas import tpu as pltpu
from jax.sharding import PartitionSpec as P

beta_one = 0.9
beta_two = 0.999
learn_rate = 0.001
adam_eps = 1e-08
bias_one = 0.9999734386011124
bias_two = 0.09520785288629115
norm_eps = 1e-06
sparsity = 1.0

MESH = pl.DeviceIdType.MESH
F32 = jnp.float32
BF16 = jnp.bfloat16

CHIPS = 8
SIDE = 4
LANES = 128
SENDS = 136
FAR_Z = (4, 3, 5, 2, 6, 1, 7)
FAR_XY = tuple(
    sorted(
        ((a, b) for a in range(SIDE) for b in range(SIDE) if a or b),
        key=lambda s: -(min(s[0], SIDE - s[0]) + min(s[1], SIDE - s[1])),
    )
)


def dot_nt(left, right):
    return lax.dot_general(
        left, right, (((1,), (1,)), ((), ())), preferred_element_type=F32
    )


def dot_tn(left, right):
    return lax.dot_general(
        left, right, (((0,), (0,)), ((), ())), preferred_element_type=F32
    )


def dot_nn(left, right):
    return jnp.dot(left, right, preferred_element_type=F32)


def adam_step(weight, moment_one, moment_two, gradient):
    first_next = beta_one * moment_one.astype(F32) + (1.0 - beta_one) * gradient
    second_next = beta_two * moment_two.astype(F32) + (1.0 - beta_two) * (gradient * gradient)
    root = bias_two**0.5
    move = (learn_rate * root / bias_one) * first_next / (jnp.sqrt(second_next) + adam_eps * root)
    stepped = weight.astype(F32) - move
    return stepped.astype(BF16), first_next.astype(BF16), second_next.astype(BF16)


def exchange_kernel(
    acts_hbm, enc_hbm, dec_hbm, m_hbm, v_hbm, ebias_ref, dbias_ref,
    tok_out, gpre_out, w_out, m_out, v_out, rsum_out,
    tok, enc, dec, dbias, lat, gside, grad, gpre,
    keep, half, rs_wide, relay, rs_z, pre,
    rb, rb_low, rs_xy, norm_lane, norm_col,
    m_old, v_old, w_new, m_new, v_new,
    load_sem, store_sem, send_sem, recv_sem,
):
    rows, width = acts_hbm.shape
    latents = enc_hbm.shape[1]
    total_rows = 2 * rows
    side = rows // 2
    piece = side // CHIPS
    lines = latents // LANES
    row_scale = sparsity / total_rows

    e, l, r = (lax.axis_index(a) for a in ("expert", "latent", "row"))
    z, c = lax.div(e, 2), lax.rem(e, 2)
    y, x = lax.div(l, 2), 2 * r + lax.rem(l, 2)

    def at_z(step):
        return lax.rem(z + step + CHIPS, CHIPS)

    def z_peer(step):
        return (at_z(step) * 2 + c, l, r)

    def at_xy(dx, dy):
        return lax.rem(x + dx, SIDE), lax.rem(y + dy, SIDE)

    def xy_peer(dx, dy):
        px, py = at_xy(dx, dy)
        return (e, py * 2 + lax.rem(px, 2), lax.div(px, 2))

    mirror_x = SIDE - 1 - x
    mirror_l, mirror_r = y * 2 + lax.rem(mirror_x, 2), lax.div(mirror_x, 2)
    other = z * 2 + 1 - c
    pair = (other, l, r)
    mirror, mirror_pair = (e, mirror_l, mirror_r), (other, mirror_l, mirror_r)

    count = [0]
    sent = []

    def send(src, dst, to):
        n = count[0]
        count[0] += 1
        copy = pltpu.make_async_remote_copy(
            src_ref=src, dst_ref=dst, send_sem=send_sem.at[n], recv_sem=recv_sem.at[n],
            device_id=to, device_id_type=MESH,
        )
        copy.start()
        sent.append(copy)
        return copy

    def arrived(copies):
        for copy in copies:
            copy.wait_recv()

    def span(start, size):
        return pl.ds(pl.multiple_of(start, size), size)

    def side_rows(h, core):
        return span(h * rows + core * side, side)

    def own_piece(h):
        return span(h * rows + c * side + z * piece, piece)

    loads = [
        pltpu.make_async_copy(src, dst, load_sem.at[n])
        for n, (src, dst) in enumerate(
            (
                (acts_hbm, tok.at[0, span(r * rows, rows)]),
                (enc_hbm, enc.at[0]), (dec_hbm, dec.at[0]),
                (m_hbm, m_old), (v_hbm, v_old),
            )
        )
    ]
    barrier = pltpu.get_barrier_semaphore()
    greeted = [
        *(z_peer(s) for s in FAR_Z), *(xy_peer(*s) for s in FAR_XY), mirror_pair, pair
    ]
    for to in greeted:
        pl.semaphore_signal(barrier, inc=1, device_id=to, device_id_type=MESH)
    for load in loads:
        load.start()
    loads[0].wait()
    loads[1].wait()
    keep[0] = dot_nn(tok[0, side_rows(r, c)], enc[0])
    dbias[0] = jnp.concatenate(
        [dbias_ref[n : n + 1, :] for n in range(width // LANES)], axis=1
    )
    loads[2].wait()
    pl.semaphore_wait(barrier, len(greeted))

    give, mine = side_rows(r, 1 - c), side_rows(r, c)
    acts_pair = send(tok.at[0, give], tok.at[1, give], pair)
    enc_pair = send(enc.at[0], enc.at[1], pair)
    acts_far = [
        send(tok.at[0, mine], tok.at[0, mine], mirror),
        send(tok.at[0, give], tok.at[1, give], mirror_pair),
    ]
    dec_pair = send(dec.at[0], dec.at[1], pair)
    bias_pair = send(dbias.at[0], dbias.at[1], pair)

    def z_part(values, step):
        return values.at[span(at_z(step) * piece, piece)]

    def z_scatter(values, slots):
        return [send(z_part(values, s), slots.at[s], z_peer(s)) for s in FAR_Z]

    def relay_start(values, slots, s):
        return [
            send(z_part(values, n), slots.at[i], z_peer(to))
            for i, (n, to) in enumerate(
                ((4 * s, -2 * s), (-3 * s, -s), (3 * s, s), (-s, -s), (s, s))
            )
        ]

    def relay_pass(values, slots, hold, copies, s):
        arrived(copies[:2])
        hold[0] = z_part(values, -2 * s)[...] + slots[0] + slots[1]
        back = send(hold.at[0], slots.at[5], z_peer(-2 * s))
        arrived(copies[2:3])
        hold[1] = z_part(values, 2 * s)[...] + slots[2]
        return [*copies[3:], back, send(hold.at[1], slots.at[6], z_peer(2 * s))]

    def z_gather(buf, h):
        at = own_piece(h)
        return [send(buf.at[at], buf.at[at], z_peer(s)) for s in FAR_Z]

    arrived([acts_pair, enc_pair])
    keep[0] = keep[0] + dot_nn(tok[1, mine], enc[1])
    first = relay_start(keep.at[0], rs_wide.at[0], 1)
    arrived(acts_far)
    theirs = side_rows(1 - r, c)
    keep[1] = dot_nn(tok[0, theirs], enc[0]) + dot_nn(tok[1, theirs], enc[1])
    second = relay_start(keep.at[1], rs_wide.at[1], -1)
    first = relay_pass(keep.at[0], rs_wide.at[0], relay.at[0], first, 1)
    second = relay_pass(keep.at[1], rs_wide.at[1], relay.at[1], second, -1)
    acts_back = send(tok.at[1, theirs], tok.at[0, theirs], pair)

    ones_lane = jnp.ones((8, width), BF16)
    ones_col = jnp.ones((width, LANES), BF16)
    arrived([dec_pair, bias_pair])
    lane, column = norm_eps, norm_eps
    for f in range(2):
        wide = dec[f].astype(F32)
        square = wide * wide
        high = square.astype(BF16)
        low = (square - high.astype(F32)).astype(BF16)
        lane = lane + (dot_nt(ones_lane, high) + dot_nt(ones_lane, low))
        column = column + (dot_nn(high, ones_col) + dot_nn(low, ones_col))
    norm_col[...] = jnp.sqrt(column)
    norm_lane[0] = jnp.sqrt(
        jnp.concatenate(
            [lane[0:1, n * LANES : (n + 1) * LANES] for n in range(lines)]
            + [jnp.zeros((8 - lines, LANES), F32)],
            axis=0,
        )
    )
    norm_copies = [send(norm_lane.at[0], norm_lane.at[s], z_peer(s)) for s in FAR_Z]
    bias = jnp.concatenate(
        [ebias_ref[pl.ds(r * lines + n, 1), :] for n in range(lines)], axis=1
    )

    def encode(k, h, copies):
        arrived(copies)
        value = keep[k, span(z * piece, piece)] + bias
        for n in range(3, 7):
            value = value + rs_wide[k, n]
        pre[h] = value
        lat[own_piece(h)] = jnp.maximum(value, 0.0).astype(BF16)
        return z_gather(lat, h)

    first = encode(0, r, first)
    second = encode(1, 1 - r, second)

    def rebuild(f, h):
        at = span(h * side, side)
        part = dot_nn(lat[side_rows(h, c)], dec[f])
        rb[f, at] = part
        rb_low[f, at] = part.astype(BF16)

    def plane_scatter(f):
        copies = []
        for dx, dy in FAR_XY:
            px, py = at_xy(dx, dy)
            at = span((px * SIDE + py) * piece, piece)
            copies.append(
                send(rb_low.at[f, at], rs_xy.at[f, dx * SIDE + dy], xy_peer(dx, dy))
            )
        return copies

    arrived(first)
    rebuild(0, r)
    arrived(second)
    rebuild(0, 1 - r)
    scatter_own = plane_scatter(0)
    rebuild(1, r)
    rebuild(1, 1 - r)
    scatter_pair = plane_scatter(1)
    lat_copies = [
        send(lat.at[side_rows(h, c)], lat.at[side_rows(h, c)], pair) for h in range(2)
    ]

    place = x * SIDE + y
    at_place = span(place * piece, piece)
    from_rows = lax.div(place, CHIPS) * rows + c * side + lax.rem(place, CHIPS) * piece

    def residual(f, copies):
        arrived(copies)
        total = rb[f, at_place]
        for n in range(1, SIDE * SIDE):
            total = total + rs_xy[f, n].astype(F32)
        acts = tok[f, span(from_rows, piece)].astype(F32)
        grad_rows = 2.0 * (total + dbias[f] - acts) / total_rows
        gside[f, at_place] = grad_rows.astype(BF16)
        ref = gside.at[f, at_place]
        return [send(ref, ref, xy_peer(*s)) for s in FAR_XY]

    gather_own = residual(0, scatter_own)
    gather_pair = residual(1, scatter_pair)
    arrived(norm_copies)
    strength = norm_lane[0]
    for s in range(1, CHIPS):
        strength = strength + norm_lane[s]
    strength = row_scale * strength
    penalty = jnp.concatenate([strength[n : n + 1, :] for n in range(lines)], axis=1)
    arrived([acts_back])
    stores = [pltpu.make_async_copy(tok.at[0], tok_out, store_sem.at[0])]
    stores[0].start()

    arrived(gather_own)
    for h in range(2):
        keep[2 + h] = dot_nt(gside[0, h * side : (h + 1) * side], dec[0])
    arrived(gather_pair)
    scatters = []
    for h in range(2):
        total = keep[2 + h] + dot_nt(gside[1, h * side : (h + 1) * side], dec[1])
        keep[2 + h] = total
        half[h] = total.astype(BF16)
        scatters.append(z_scatter(half.at[h], rs_z.at[h]))

    grad_copies = [
        send(gside.at[1, span(h * side, side)], grad.at[side_rows(h, c)], pair)
        for h in range(2)
    ]
    for h in range(2):
        grad[side_rows(h, c)] = gside[0, h * side : (h + 1) * side]
    loads[3].wait()
    loads[4].wait()
    arrived(lat_copies)
    arrived(grad_copies)
    ones_rows = jnp.ones((total_rows, LANES), BF16)

    def decoder_block(n, carry):
        at = span(n * LANES, LANES)
        acts = lat[:, at]
        gradient = dot_tn(acts, grad[...])
        factor = row_scale * dot_tn(acts, ones_rows) / norm_col[at]
        weight = dec[0, at]
        gradient = gradient + jnp.tile(factor, (1, width // LANES)) * weight.astype(F32)
        w_new[at], m_new[at], v_new[at] = adam_step(weight, m_old[at], v_old[at], gradient)
        return carry

    lax.fori_loop(0, lines // 2, decoder_block, 0)

    def back(h, copies):
        arrived(copies)
        value = keep[2 + h, span(z * piece, piece)] + penalty
        for s in range(1, CHIPS):
            value = value + rs_z[h, s].astype(F32)
        gpre[own_piece(h)] = jnp.where(pre[h] > 0, value, 0.0).astype(BF16)
        return z_gather(gpre, h)

    gathers = [back(h, scatters[h]) for h in range(2)]
    lax.fori_loop(lines // 2, lines, decoder_block, 0)
    stores += [
        pltpu.make_async_copy(w_new, w_out, store_sem.at[1]),
        pltpu.make_async_copy(m_new, m_out, store_sem.at[2]),
        pltpu.make_async_copy(v_new, v_out, store_sem.at[3]),
    ]
    for store in stores[1:]:
        store.start()
    row_sum = dot_nn(jnp.ones((8, total_rows), BF16), grad[...])
    rsum_out[...] = jnp.concatenate(
        [row_sum[0:1, n * LANES : (n + 1) * LANES] for n in range(width // LANES)], axis=0
    )
    last = []
    for h in range(2):
        arrived(gathers[h])
        ref = gpre.at[side_rows(h, c)]
        last.append(send(ref, ref, pair))
    arrived(last)
    stores.append(pltpu.make_async_copy(gpre, gpre_out, store_sem.at[4]))
    stores[-1].start()
    for copy in sent:
        copy.wait_send()
    for store in stores:
        store.wait()
    assert count[0] == SENDS


def exchange(acts, enc_weight, dec_weight, dec_first, dec_second, enc_bias, dec_bias):
    rows, width = acts.shape
    latents = enc_weight.shape[1]
    total_rows = 2 * rows
    side = rows // 2
    piece = side // CHIPS
    hbm = pl.BlockSpec(memory_space=pltpu.HBM)
    vmem = pl.BlockSpec(memory_space=pltpu.VMEM)
    dec_shape = (latents, width)
    return pl.pallas_call(
        exchange_kernel,
        name="exchange",
        out_shape=(
            jax.ShapeDtypeStruct((total_rows, width), BF16),
            jax.ShapeDtypeStruct((total_rows, latents), BF16),
            jax.ShapeDtypeStruct(dec_shape, BF16),
            jax.ShapeDtypeStruct(dec_shape, BF16),
            jax.ShapeDtypeStruct(dec_shape, BF16),
            jax.ShapeDtypeStruct((width // LANES, LANES), F32),
        ),
        in_specs=[hbm] * 5 + [vmem] * 2,
        out_specs=(hbm,) * 5 + (vmem,),
        scratch_shapes=[
            pltpu.VMEM((2, total_rows, width), BF16),
            pltpu.VMEM((2, width, latents), BF16),
            pltpu.VMEM((2, *dec_shape), BF16),
            pltpu.VMEM((2, 1, width), F32),
            pltpu.VMEM((total_rows, latents), BF16),
            pltpu.VMEM((2, rows, width), BF16),
            pltpu.VMEM((total_rows, width), BF16),
            pltpu.VMEM((total_rows, latents), BF16),
            pltpu.VMEM((4, side, latents), F32),
            pltpu.VMEM((2, side, latents), BF16),
            pltpu.VMEM((2, 7, piece, latents), F32),
            pltpu.VMEM((2, 2, piece, latents), F32),
            pltpu.VMEM((2, CHIPS, piece, latents), BF16),
            pltpu.VMEM((2, piece, latents), F32),
            pltpu.VMEM((2, rows, width), F32),
            pltpu.VMEM((2, rows, width), BF16),
            pltpu.VMEM((2, SIDE * SIDE, piece, width), BF16),
            pltpu.VMEM((CHIPS, 8, LANES), F32),
            pltpu.VMEM((latents, LANES), F32),
            *[pltpu.VMEM(dec_shape, BF16)] * 5,
            pltpu.SemaphoreType.DMA((5,)),
            pltpu.SemaphoreType.DMA((5,)),
            pltpu.SemaphoreType.DMA((SENDS,)),
            pltpu.SemaphoreType.DMA((SENDS,)),
        ],
        compiler_params=pltpu.CompilerParams(
            collective_id=0, has_side_effects=True, vmem_limit_bytes=60 << 20
        ),
    )(acts, enc_weight, dec_weight, dec_first, dec_second, enc_bias, dec_bias)


def finish_kernel(
    tok_ref, gpre_ref, w, m, v, rsum_ref, w_done, m_done, v_done,
    w_next, m_next, v_next, bsum_out, rsum_out, w_out, m_out, v_out,
):
    @pl.when(pl.program_id(0) == 0)
    def _():
        total = dot_nn(jnp.ones((8, gpre_ref.shape[0]), BF16), gpre_ref[...])
        for n in range(bsum_out.shape[0]):
            bsum_out[n : n + 1, :] = total[0:1, n * LANES : (n + 1) * LANES]
        rsum_out[...] = rsum_ref[...]

    gradient = dot_tn(tok_ref[...], gpre_ref[...])
    w_next[...], m_next[...], v_next[...] = adam_step(w[...], m[...], v[...], gradient)
    w_out[...] = w_done[...]
    m_out[...] = m_done[...]
    v_out[...] = v_done[...]


def finish(tok, gpre, w, m, v, row_sum, decoder, blocks=4):
    total_rows, latents = gpre.shape
    width = w.shape[0]
    block = pl.BlockSpec((width // blocks, latents), lambda i: (i, 0))
    turned = pl.BlockSpec((latents // blocks, width), lambda i: (i, 0))

    def whole(shape):
        return pl.BlockSpec(shape, lambda i: (0, 0))

    shapes = (latents // LANES, LANES), (width // LANES, LANES)
    return pl.pallas_call(
        finish_kernel,
        name="finish",
        grid=(blocks,),
        out_shape=(jax.ShapeDtypeStruct(w.shape, BF16),) * 3
        + tuple(jax.ShapeDtypeStruct(s, F32) for s in shapes)
        + (jax.ShapeDtypeStruct(decoder[0].shape, BF16),) * 3,
        in_specs=[
            pl.BlockSpec((total_rows, width // blocks), lambda i: (0, i)),
            whole((total_rows, latents)), block, block, block, whole(shapes[1]),
            turned, turned, turned,
        ],
        out_specs=(block,) * 3 + tuple(whole(s) for s in shapes) + (turned,) * 3,
        compiler_params=pltpu.CompilerParams(vmem_limit_bytes=56 << 20),
    )(tok, gpre, w, m, v, row_sum, *decoder)


def local(
    model_acts, enc_weight, dec_weight, enc_bias, dec_bias,
    enc_first, enc_second, dec_first, dec_second,
):
    tok, gpre, *decoder, row_sum = exchange(
        model_acts, enc_weight, dec_weight, dec_first, dec_second,
        enc_bias.reshape(-1, LANES), dec_bias.reshape(-1, LANES),
    )
    encoder = finish(tok, gpre, enc_weight, enc_first, enc_second, row_sum, decoder)
    enc_next, enc_m, enc_v, bias_sum, row_sum, dec_next, dec_m, dec_v = encoder
    return (
        enc_next, dec_next, enc_m, enc_v, dec_m, dec_v,
        bias_sum.reshape(-1), row_sum.reshape(-1),
    )


def solution(mesh):
    split = P("expert", ("latent", "row"))
    turned = P(("latent", "row"), "expert")
    return jax.shard_map(
        local,
        mesh=mesh,
        in_specs=(
            P("row", "expert"), split, turned, P("latent"), P("expert"),
            split, split, turned, turned,
        ),
        out_specs=(
            split, turned, split, split, turned, turned,
            P(("latent", "row")), P("expert"),
        ),
        check_vma=False,
    )
```

```python
import functools

import jax
import jax.numpy as jnp
from jax import lax
from jax.experimental import pallas as pl
from jax.experimental.pallas import tpu as pltpu
from jax.sharding import PartitionSpec as P

beta_one = 0.9
beta_two = 0.999
learn_rate = 0.001
adam_eps = 1e-08
bias_one = 0.9999734386011124
bias_two = 0.09520785288629115
norm_eps = 1e-06
sparsity = 1.0

MESH = pl.DeviceIdType.MESH
F32 = jnp.float32
BF16 = jnp.bfloat16

CHIPS = 8
SIDE = 4
LANES = 128
SENDS = 136
FAR_Z = (4, 3, 5, 2, 6, 1, 7)
FAR_XY = tuple(
    sorted(
        ((a, b) for a in range(SIDE) for b in range(SIDE) if a or b),
        key=lambda s: -(min(s[0], SIDE - s[0]) + min(s[1], SIDE - s[1])),
    )
)


def dot_nt(left, right):
    return lax.dot_general(
        left, right, (((1,), (1,)), ((), ())), preferred_element_type=F32
    )


def dot_tn(left, right):
    return lax.dot_general(
        left, right, (((0,), (0,)), ((), ())), preferred_element_type=F32
    )


def dot_nn(left, right):
    return jnp.dot(left, right, preferred_element_type=F32)


def adam_step(weight, moment_one, moment_two, gradient):
    first_next = beta_one * moment_one.astype(F32) + (1.0 - beta_one) * gradient
    second_next = beta_two * moment_two.astype(F32) + (1.0 - beta_two) * (gradient * gradient)
    root = bias_two**0.5
    move = (learn_rate * root / bias_one) * first_next / (jnp.sqrt(second_next) + adam_eps * root)
    stepped = weight.astype(F32) - move
    return stepped.astype(BF16), first_next.astype(BF16), second_next.astype(BF16)


def exchange_kernel(
    acts_hbm, enc_hbm, dec_hbm, dec_m_hbm, dec_v_hbm, enc_m_hbm, enc_v_hbm,
    ebias_hbm, dbias_hbm,
    tok_out, gpre_out, w_new, m_new, v_new, enc_out, enc_m_out, enc_v_out, rsum_out,
    tok, enc, dec, dbias, lat, gside, grad, gpre,
    keep, half, rs_wide, relay, rs_z, pre,
    rb, rb_low, rs_xy, norm_lane, norm_col,
    m_old, v_old, ebias_ref, dbias_ref, load_sem, send_sem, recv_sem,
):
    rows, width = acts_hbm.shape
    latents = enc_hbm.shape[1]
    total_rows = 2 * rows
    side = rows // 2
    piece = side // CHIPS
    lines = latents // LANES
    row_scale = sparsity / total_rows

    e, l, r = (lax.axis_index(a) for a in ("expert", "latent", "row"))
    z, c = lax.div(e, 2), lax.rem(e, 2)
    y, x = lax.div(l, 2), 2 * r + lax.rem(l, 2)

    def at_z(step):
        return lax.rem(z + step + CHIPS, CHIPS)

    def z_peer(step):
        return (at_z(step) * 2 + c, l, r)

    def at_xy(dx, dy):
        return lax.rem(x + dx, SIDE), lax.rem(y + dy, SIDE)

    def xy_peer(dx, dy):
        px, py = at_xy(dx, dy)
        return (e, py * 2 + lax.rem(px, 2), lax.div(px, 2))

    mirror_x = SIDE - 1 - x
    mirror_l, mirror_r = y * 2 + lax.rem(mirror_x, 2), lax.div(mirror_x, 2)
    other = z * 2 + 1 - c
    pair = (other, l, r)
    mirror, mirror_pair = (e, mirror_l, mirror_r), (other, mirror_l, mirror_r)

    count = [0]
    sent = []

    def send(src, dst, to):
        n = count[0]
        count[0] += 1
        copy = pltpu.make_async_remote_copy(
            src_ref=src, dst_ref=dst, send_sem=send_sem.at[n], recv_sem=recv_sem.at[n],
            device_id=to, device_id_type=MESH,
        )
        copy.start()
        sent.append(copy)
        return copy

    def arrived(copies):
        for copy in copies:
            copy.wait_recv()

    def span(start, size):
        return pl.ds(pl.multiple_of(start, size), size)

    def side_rows(h, core):
        return span(h * rows + core * side, side)

    def own_piece(h):
        return span(h * rows + c * side + z * piece, piece)

    loads = [
        pltpu.make_async_copy(src, dst, load_sem.at[n])
        for n, (src, dst) in enumerate(
            (
                (acts_hbm, tok.at[0, span(r * rows, rows)]),
                (enc_hbm, enc.at[0]), (dec_hbm, dec.at[0]),
                (dec_m_hbm, m_old), (dec_v_hbm, v_old), (enc_hbm, enc_out),
                (enc_m_hbm, enc_m_out), (enc_v_hbm, enc_v_out), (ebias_hbm, ebias_ref),
                (dbias_hbm, dbias_ref),
            )
        )
    ]
    barrier = pltpu.get_barrier_semaphore()
    greeted = [
        *(z_peer(s) for s in FAR_Z), *(xy_peer(*s) for s in FAR_XY), mirror_pair, pair
    ]
    for to in greeted:
        pl.semaphore_signal(barrier, inc=1, device_id=to, device_id_type=MESH)
    for load in loads[:3]:
        load.start()
    for load in loads[8:]:
        load.start()
    loads[0].wait()
    loads[1].wait()
    keep[0] = dot_nn(tok[0, side_rows(r, c)], enc[0])
    for load in loads[8:]:
        load.wait()
    dbias[0] = jnp.concatenate(
        [dbias_ref[n : n + 1, :] for n in range(width // LANES)], axis=1
    )
    loads[2].wait()
    for load in loads[3:8]:
        load.start()
    pl.semaphore_wait(barrier, len(greeted))

    give, mine = side_rows(r, 1 - c), side_rows(r, c)
    acts_pair = send(tok.at[0, give], tok.at[1, give], pair)
    enc_pair = send(enc.at[0], enc.at[1], pair)
    acts_far = [
        send(tok.at[0, mine], tok.at[0, mine], mirror),
        send(tok.at[0, give], tok.at[1, give], mirror_pair),
    ]
    dec_pair = send(dec.at[0], dec.at[1], pair)
    bias_pair = send(dbias.at[0], dbias.at[1], pair)

    def z_part(values, step):
        return values.at[span(at_z(step) * piece, piece)]

    def z_scatter(values, slots):
        return [send(z_part(values, s), slots.at[s], z_peer(s)) for s in FAR_Z]

    def relay_start(values, slots, s):
        return [
            send(z_part(values, n), slots.at[i], z_peer(to))
            for i, (n, to) in enumerate(
                ((4 * s, -2 * s), (-3 * s, -s), (3 * s, s), (-s, -s), (s, s))
            )
        ]

    def relay_pass(values, slots, hold, copies, s):
        arrived(copies[:2])
        hold[0] = z_part(values, -2 * s)[...] + slots[0] + slots[1]
        back = send(hold.at[0], slots.at[5], z_peer(-2 * s))
        arrived(copies[2:3])
        hold[1] = z_part(values, 2 * s)[...] + slots[2]
        return [*copies[3:], back, send(hold.at[1], slots.at[6], z_peer(2 * s))]

    def z_gather(buf, h):
        at = own_piece(h)
        return [send(buf.at[at], buf.at[at], z_peer(s)) for s in FAR_Z]

    arrived([acts_pair, enc_pair])
    keep[0] = keep[0] + dot_nn(tok[1, mine], enc[1])
    first = relay_start(keep.at[0], rs_wide.at[0], 1)
    arrived(acts_far)
    theirs = side_rows(1 - r, c)
    keep[1] = dot_nn(tok[0, theirs], enc[0]) + dot_nn(tok[1, theirs], enc[1])
    second = relay_start(keep.at[1], rs_wide.at[1], -1)
    first = relay_pass(keep.at[0], rs_wide.at[0], relay.at[0], first, 1)
    second = relay_pass(keep.at[1], rs_wide.at[1], relay.at[1], second, -1)
    acts_back = send(tok.at[1, theirs], tok.at[0, theirs], pair)

    ones_lane = jnp.ones((8, width), BF16)
    ones_col = jnp.ones((width, LANES), BF16)
    arrived([dec_pair, bias_pair])
    lane, column = norm_eps, norm_eps
    for f in range(2):
        wide = dec[f].astype(F32)
        square = wide * wide
        high = square.astype(BF16)
        low = (square - high.astype(F32)).astype(BF16)
        lane = lane + (dot_nt(ones_lane, high) + dot_nt(ones_lane, low))
        column = column + (dot_nn(high, ones_col) + dot_nn(low, ones_col))
    norm_col[...] = jnp.sqrt(column)
    norm_lane[0] = jnp.sqrt(
        jnp.concatenate(
            [lane[0:1, n * LANES : (n + 1) * LANES] for n in range(lines)]
            + [jnp.zeros((8 - lines, LANES), F32)],
            axis=0,
        )
    )
    norm_copies = [send(norm_lane.at[0], norm_lane.at[s], z_peer(s)) for s in FAR_Z]
    bias = jnp.concatenate(
        [ebias_ref[pl.ds(r * lines + n, 1), :] for n in range(lines)], axis=1
    )

    def encode(k, h, copies):
        arrived(copies)
        value = keep[k, span(z * piece, piece)] + bias
        for n in range(3, 7):
            value = value + rs_wide[k, n]
        pre[h] = value
        lat[own_piece(h)] = jnp.maximum(value, 0.0).astype(BF16)
        return z_gather(lat, h)

    first = encode(0, r, first)
    second = encode(1, 1 - r, second)

    def rebuild(f, h):
        at = span(h * side, side)
        part = dot_nn(lat[side_rows(h, c)], dec[f])
        rb[f, at] = part
        rb_low[f, at] = part.astype(BF16)

    def plane_scatter(f):
        copies = []
        for dx, dy in FAR_XY:
            px, py = at_xy(dx, dy)
            at = span((px * SIDE + py) * piece, piece)
            copies.append(
                send(rb_low.at[f, at], rs_xy.at[f, dx * SIDE + dy], xy_peer(dx, dy))
            )
        return copies

    arrived(first)
    rebuild(0, r)
    arrived(second)
    rebuild(0, 1 - r)
    scatter_own = plane_scatter(0)
    rebuild(1, r)
    rebuild(1, 1 - r)
    scatter_pair = plane_scatter(1)
    lat_copies = [
        send(lat.at[side_rows(h, c)], lat.at[side_rows(h, c)], pair) for h in range(2)
    ]

    place = x * SIDE + y
    at_place = span(place * piece, piece)
    from_rows = lax.div(place, CHIPS) * rows + c * side + lax.rem(place, CHIPS) * piece

    def residual(f, copies):
        arrived(copies)
        total = rb[f, at_place]
        for n in range(1, SIDE * SIDE):
            total = total + rs_xy[f, n].astype(F32)
        acts = tok[f, span(from_rows, piece)].astype(F32)
        grad_rows = 2.0 * (total + dbias[f] - acts) / total_rows
        gside[f, at_place] = grad_rows.astype(BF16)
        ref = gside.at[f, at_place]
        return [send(ref, ref, xy_peer(*s)) for s in FAR_XY]

    gather_own = residual(0, scatter_own)
    gather_pair = residual(1, scatter_pair)
    arrived(norm_copies)
    strength = norm_lane[0]
    for s in range(1, CHIPS):
        strength = strength + norm_lane[s]
    strength = row_scale * strength
    penalty = jnp.concatenate([strength[n : n + 1, :] for n in range(lines)], axis=1)
    arrived([acts_back])
    tok_out[...] = tok[0]

    arrived(gather_own)
    for h in range(2):
        keep[2 + h] = dot_nt(gside[0, h * side : (h + 1) * side], dec[0])
    arrived(gather_pair)
    scatters = []
    for h in range(2):
        total = keep[2 + h] + dot_nt(gside[1, h * side : (h + 1) * side], dec[1])
        keep[2 + h] = total
        half[h] = total.astype(BF16)
        scatters.append(z_scatter(half.at[h], rs_z.at[h]))

    grad_copies = [
        send(gside.at[1, span(h * side, side)], grad.at[side_rows(h, c)], pair)
        for h in range(2)
    ]
    for h in range(2):
        grad[side_rows(h, c)] = gside[0, h * side : (h + 1) * side]
    for load in loads[3:8]:
        load.wait()
    arrived(lat_copies)
    arrived(grad_copies)
    ones_rows = jnp.ones((total_rows, LANES), BF16)

    def decoder_block(n, carry):
        at = span(n * LANES, LANES)
        acts = lat[:, at]
        gradient = dot_tn(acts, grad[...])
        factor = row_scale * dot_tn(acts, ones_rows) / norm_col[at]
        weight = dec[0, at]
        gradient = gradient + jnp.tile(factor, (1, width // LANES)) * weight.astype(F32)
        w_new[at], m_new[at], v_new[at] = adam_step(weight, m_old[at], v_old[at], gradient)
        return carry

    lax.fori_loop(0, lines // 2, decoder_block, 0)

    def back(h, copies):
        arrived(copies)
        value = keep[2 + h, span(z * piece, piece)] + penalty
        for s in range(1, CHIPS):
            value = value + rs_z[h, s].astype(F32)
        gpre[own_piece(h)] = jnp.where(pre[h] > 0, value, 0.0).astype(BF16)
        return z_gather(gpre, h)

    gathers = [back(h, scatters[h]) for h in range(2)]
    lax.fori_loop(lines // 2, lines, decoder_block, 0)
    row_sum = dot_nn(jnp.ones((8, total_rows), BF16), grad[...])
    rsum_out[...] = jnp.concatenate(
        [row_sum[0:1, n * LANES : (n + 1) * LANES] for n in range(width // LANES)], axis=0
    )
    last = []
    for h in range(2):
        arrived(gathers[h])
        ref = gpre.at[side_rows(h, c)]
        last.append(send(ref, ref, pair))
    for h in range(2):
        gpre_out[side_rows(h, c)] = gpre[side_rows(h, c)]
    for copy in sent:
        copy.wait_send()
    for h in range(2):
        arrived(last[h : h + 1])
        gpre_out[side_rows(h, 1 - c)] = gpre[side_rows(h, 1 - c)]
    assert count[0] == SENDS


def exchange(acts, enc_weight, dec_weight, dec_m, dec_v, enc_m, enc_v, enc_bias, dec_bias):
    rows, width = acts.shape
    latents = enc_weight.shape[1]
    total_rows = 2 * rows
    side = rows // 2
    piece = side // CHIPS
    hbm = pl.BlockSpec(memory_space=pltpu.HBM)
    vmem = pl.BlockSpec(memory_space=pltpu.VMEM)
    dec_shape = (latents, width)
    return pl.pallas_call(
        exchange_kernel,
        name="exchange",
        out_shape=(
            jax.ShapeDtypeStruct((total_rows, width), BF16),
            jax.ShapeDtypeStruct((total_rows, latents), BF16),
            *[jax.ShapeDtypeStruct(dec_shape, BF16)] * 3,
            *[jax.ShapeDtypeStruct(enc_weight.shape, BF16)] * 3,
            jax.ShapeDtypeStruct((width // LANES, LANES), F32),
        ),
        in_specs=[hbm] * 9,
        out_specs=(vmem,) * 9,
        scratch_shapes=[
            pltpu.VMEM((2, total_rows, width), BF16),
            pltpu.VMEM((2, width, latents), BF16),
            pltpu.VMEM((2, *dec_shape), BF16),
            pltpu.VMEM((2, 1, width), F32),
            pltpu.VMEM((total_rows, latents), BF16),
            pltpu.VMEM((2, rows, width), BF16),
            pltpu.VMEM((total_rows, width), BF16),
            pltpu.VMEM((total_rows, latents), BF16),
            pltpu.VMEM((4, side, latents), F32),
            pltpu.VMEM((2, side, latents), BF16),
            pltpu.VMEM((2, 7, piece, latents), F32),
            pltpu.VMEM((2, 2, piece, latents), F32),
            pltpu.VMEM((2, CHIPS, piece, latents), BF16),
            pltpu.VMEM((2, piece, latents), F32),
            pltpu.VMEM((2, rows, width), F32),
            pltpu.VMEM((2, rows, width), BF16),
            pltpu.VMEM((2, SIDE * SIDE, piece, width), BF16),
            pltpu.VMEM((CHIPS, 8, LANES), F32),
            pltpu.VMEM((latents, LANES), F32),
            *[pltpu.VMEM(dec_shape, BF16)] * 2,
            pltpu.VMEM(enc_bias.shape, F32),
            pltpu.VMEM(dec_bias.shape, F32),
            pltpu.SemaphoreType.DMA((10,)),
            pltpu.SemaphoreType.DMA((SENDS,)),
            pltpu.SemaphoreType.DMA((SENDS,)),
        ],
        compiler_params=pltpu.CompilerParams(
            collective_id=0, has_side_effects=True, vmem_limit_bytes=30 << 20
        ),
    )(acts, enc_weight, dec_weight, dec_m, dec_v, enc_m, enc_v, enc_bias, dec_bias)


def finish_kernel(
    tok_ref, gpre_ref, w_done, m_done, v_done, w, m, v, rsum_ref,
    w_next, m_next, v_next, bsum_out, rsum_out, w_out, m_out, v_out, sem,
):
    blocks = pl.num_programs(0)
    step = pl.program_id(0)
    copies = [
        pltpu.make_async_copy(src, dst, sem.at[n])
        for n, (src, dst) in enumerate(((w_done, w_out), (m_done, m_out), (v_done, v_out)))
    ]

    @pl.when(step == 0)
    def _():
        for copy in copies:
            copy.start()
        total = dot_nn(jnp.ones((8, gpre_ref.shape[0]), BF16), gpre_ref[...])
        for n in range(bsum_out.shape[0]):
            bsum_out[n : n + 1, :] = total[0:1, n * LANES : (n + 1) * LANES]
        rsum_out[...] = rsum_ref[...]

    size = w_next.shape[0]
    at = pl.ds(pl.multiple_of(step * size, size), size)
    gradient = dot_tn(tok_ref[:, at], gpre_ref[...])
    w_next[...], m_next[...], v_next[...] = adam_step(w[at], m[at], v[at], gradient)

    @pl.when(step == blocks - 1)
    def _():
        for copy in copies:
            copy.wait()


def finish(tok, gpre, decoder, encoder, row_sum, blocks=4):
    latents, width = decoder[0].shape
    block = pl.BlockSpec((width // blocks, latents), lambda i: (i, 0))
    vmem = pl.BlockSpec(memory_space=pltpu.VMEM)
    hbm = pl.BlockSpec(memory_space=pltpu.HBM)

    def whole(shape):
        return pl.BlockSpec(shape, lambda i: (0, 0))

    shapes = (latents // LANES, LANES), (width // LANES, LANES)
    return pl.pallas_call(
        finish_kernel,
        name="finish",
        grid=(blocks,),
        out_shape=(jax.ShapeDtypeStruct((width, latents), BF16),) * 3
        + tuple(jax.ShapeDtypeStruct(s, F32) for s in shapes)
        + (jax.ShapeDtypeStruct((latents, width), BF16),) * 3,
        in_specs=[vmem] * 9,
        out_specs=(block,) * 3 + tuple(whole(s) for s in shapes) + (hbm,) * 3,
        scratch_shapes=[pltpu.SemaphoreType.DMA((3,))],
        compiler_params=pltpu.CompilerParams(vmem_limit_bytes=40 << 20),
    )(tok, gpre, *decoder, *encoder, row_sum)


def local(
    model_acts, enc_weight, dec_weight, enc_bias, dec_bias,
    enc_first, enc_second, dec_first, dec_second,
):
    moments = dec_first, dec_second, enc_first, enc_second
    biases = enc_bias.reshape(-1, LANES), dec_bias.reshape(-1, LANES)
    results = exchange(
        *(
            pltpu.with_memory_space_constraint(a, pltpu.HBM)
            for a in (model_acts, enc_weight, dec_weight, *moments, *biases)
        )
    )
    tok, gpre, row_sum = results[0], results[1], results[8]
    enc_next, enc_m, enc_v, bias_sum, row_sum, dec_next, dec_m, dec_v = finish(
        tok, gpre, results[2:5], results[5:8], row_sum
    )
    return (
        enc_next, dec_next, enc_m, enc_v, dec_m, dec_v,
        bias_sum.reshape(-1), row_sum.reshape(-1),
    )


def solution(mesh):
    split = P("expert", ("latent", "row"))
    turned = P(("latent", "row"), "expert")
    return jax.shard_map(
        local,
        mesh=mesh,
        in_specs=(
            P("row", "expert"), split, turned, P("latent"), P("expert"),
            split, split, turned, turned,
        ),
        out_specs=(
            split, turned, split, split, turned, turned,
            P(("latent", "row")), P("expert"),
        ),
        check_vma=False,
    )
```

```python
import functools

import jax
import jax.numpy as jnp
from jax import lax
from jax.experimental import pallas as pl
from jax.experimental.pallas import tpu as pltpu
from jax.sharding import PartitionSpec as P

beta_one = 0.9
beta_two = 0.999
learn_rate = 0.001
adam_eps = 1e-08
bias_one = 0.9999734386011124
bias_two = 0.09520785288629115
norm_eps = 1e-06
sparsity = 1.0

MESH = pl.DeviceIdType.MESH
F32 = jnp.float32
BF16 = jnp.bfloat16

CHIPS = 8
SIDE = 4
LANES = 128
SENDS = 136
EARLY, LATE = 2, 5
FAR_Z = (4, 3, 5, 2, 6, 1, 7)
FAR_XY = tuple(
    sorted(
        ((a, b) for a in range(SIDE) for b in range(SIDE) if a or b),
        key=lambda s: -(min(s[0], SIDE - s[0]) + min(s[1], SIDE - s[1])),
    )
)


def dot_nt(left, right):
    return lax.dot_general(
        left, right, (((1,), (1,)), ((), ())), preferred_element_type=F32
    )


def dot_tn(left, right):
    return lax.dot_general(
        left, right, (((0,), (0,)), ((), ())), preferred_element_type=F32
    )


def dot_nn(left, right):
    return jnp.dot(left, right, preferred_element_type=F32)


def adam_step(weight, moment_one, moment_two, gradient):
    first_next = beta_one * moment_one.astype(F32) + (1.0 - beta_one) * gradient
    second_next = beta_two * moment_two.astype(F32) + (1.0 - beta_two) * (gradient * gradient)
    root = bias_two**0.5
    move = (learn_rate * root / bias_one) * first_next / (jnp.sqrt(second_next) + adam_eps * root)
    stepped = weight.astype(F32) - move
    return stepped.astype(BF16), first_next.astype(BF16), second_next.astype(BF16)


def exchange_kernel(
    acts_hbm, enc_hbm, dec_hbm, dec_m_hbm, dec_v_hbm, enc_m_hbm, enc_v_hbm,
    ebias_hbm, dbias_hbm,
    tok_out, gpre_out, w_new, m_new, v_new, enc_out, enc_m_out, enc_v_out, rsum_out,
    tok, enc, dec, dbias, lat, gside, grad, gpre,
    keep, half, rs_wide, relay, rs_z, pre,
    rb, rb_low, rs_xy, norm_lane, norm_col,
    m_old, v_old, ebias_ref, dbias_ref, load_sem, send_sem, recv_sem,
):
    rows, width = acts_hbm.shape
    latents = enc_hbm.shape[1]
    total_rows = 2 * rows
    side = rows // 2
    piece = side // CHIPS
    lines = latents // LANES
    part = 2 * side // (SIDE * SIDE)
    row_scale = sparsity / total_rows

    e, l, r = (lax.axis_index(a) for a in ("expert", "latent", "row"))
    z, c = lax.div(e, 2), lax.rem(e, 2)
    y, x = lax.div(l, 2), 2 * r + lax.rem(l, 2)

    def at_z(step):
        return lax.rem(z + step + CHIPS, CHIPS)

    def z_peer(step):
        return (at_z(step) * 2 + c, l, r)

    def at_xy(dx, dy):
        return lax.rem(x + dx, SIDE), lax.rem(y + dy, SIDE)

    def xy_peer(dx, dy):
        px, py = at_xy(dx, dy)
        return (e, py * 2 + lax.rem(px, 2), lax.div(px, 2))

    mirror_x = SIDE - 1 - x
    mirror_l, mirror_r = y * 2 + lax.rem(mirror_x, 2), lax.div(mirror_x, 2)
    other = z * 2 + 1 - c
    pair = (other, l, r)
    mirror, mirror_pair = (e, mirror_l, mirror_r), (other, mirror_l, mirror_r)

    count = [0]
    sent = []

    def send(src, dst, to):
        n = count[0]
        count[0] += 1
        copy = pltpu.make_async_remote_copy(
            src_ref=src, dst_ref=dst, send_sem=send_sem.at[n], recv_sem=recv_sem.at[n],
            device_id=to, device_id_type=MESH,
        )
        copy.start()
        sent.append(copy)
        return copy

    def arrived(copies):
        for copy in copies:
            copy.wait_recv()

    def span(start, size):
        return pl.ds(pl.multiple_of(start, size), size)

    def side_rows(h, core):
        return span(h * rows + core * side, side)

    def own_piece(h):
        return span(h * rows + c * side + z * piece, piece)

    loads = [
        pltpu.make_async_copy(src, dst, load_sem.at[n])
        for n, (src, dst) in enumerate(
            (
                (acts_hbm, tok.at[0, span(r * rows, rows)]),
                (enc_hbm, enc.at[0]), (dec_hbm, dec.at[0]),
                (dec_m_hbm, m_old), (dec_v_hbm, v_old), (enc_hbm, enc_out),
                (enc_m_hbm, enc_m_out), (enc_v_hbm, enc_v_out), (ebias_hbm, ebias_ref),
                (dbias_hbm, dbias_ref),
            )
        )
    ]
    barrier = pltpu.get_barrier_semaphore()
    greeted = [
        *(z_peer(s) for s in FAR_Z), *(xy_peer(*s) for s in FAR_XY), mirror_pair, pair
    ]
    for to in greeted:
        pl.semaphore_signal(barrier, inc=1, device_id=to, device_id_type=MESH)
    for load in loads[:3] + loads[8:]:
        load.start()
    pl.semaphore_wait(barrier, len(greeted))

    give = side_rows(r, 1 - c)
    give_hbm = acts_hbm.at[span((1 - c) * side, side)]
    acts_far = [
        send(acts_hbm.at[span(c * side, side)], tok.at[0, side_rows(r, c)], mirror),
        send(give_hbm, tok.at[1, give], mirror_pair),
    ]
    acts_pair = send(give_hbm, tok.at[1, give], pair)
    enc_pair = send(enc_hbm, enc.at[1], pair)
    for load in loads[3:8]:
        load.start()
    for load in loads[8:]:
        load.wait()
    dbias[0] = jnp.concatenate(
        [dbias_ref[n : n + 1, :] for n in range(width // LANES)], axis=1
    )
    for load in loads[:2]:
        load.wait()

    ones_lane = jnp.ones((8, width), BF16)
    ones_col = jnp.ones((width, LANES), BF16)

    def squares(f):
        wide = dec[f].astype(F32)
        square = wide * wide
        high = square.astype(BF16)
        low = (square - high.astype(F32)).astype(BF16)
        return (
            dot_nt(ones_lane, high) + dot_nt(ones_lane, low),
            dot_nn(high, ones_col) + dot_nn(low, ones_col),
        )

    def z_part(values, step):
        return values.at[span(at_z(step) * piece, piece)]

    def z_scatter(values, slots):
        return [send(z_part(values, s), slots.at[s], z_peer(s)) for s in FAR_Z]

    def relay_start(values, slots, s):
        return [
            send(z_part(values, n), slots.at[i], z_peer(to))
            for i, (n, to) in enumerate(
                ((4 * s, -2 * s), (-3 * s, -s), (3 * s, s), (-s, -s), (s, s))
            )
        ]

    def relay_pass(values, slots, hold, copies, s):
        arrived(copies[:2])
        hold[0] = z_part(values, -2 * s)[...] + slots[0] + slots[1]
        back = send(hold.at[0], slots.at[5], z_peer(-2 * s))
        arrived(copies[2:3])
        hold[1] = z_part(values, 2 * s)[...] + slots[2]
        return [*copies[3:], back, send(hold.at[1], slots.at[6], z_peer(2 * s))]

    def z_gather(buf, h):
        at = own_piece(h)
        return [send(buf.at[at], buf.at[at], z_peer(s)) for s in FAR_Z]

    arrived([acts_pair, enc_pair, *acts_far])
    encoded = []
    for h, s in enumerate((1, -1)):
        at = side_rows(h, c)
        keep[h] = dot_nn(tok[0, at], enc[0]) + dot_nn(tok[1, at], enc[1])
        encoded.append(relay_start(keep.at[h], rs_wide.at[h], s))
    bias_pair = send(dbias.at[0], dbias.at[1], pair)
    dec_pair = send(dec_hbm, dec.at[1], pair)
    loads[2].wait()
    theirs = side_rows(1 - r, c)
    acts_back = send(tok.at[1, theirs], tok.at[0, theirs], pair)
    for h, s in enumerate((1, -1)):
        encoded[h] = relay_pass(keep.at[h], rs_wide.at[h], relay.at[h], encoded[h], s)

    lane, column = squares(0)
    arrived([dec_pair, bias_pair])
    more_lane, more_column = squares(1)
    lane = lane + more_lane + norm_eps
    norm_col[...] = jnp.sqrt(column + more_column + norm_eps)
    norm_lane[0] = jnp.sqrt(
        jnp.concatenate(
            [lane[0:1, n * LANES : (n + 1) * LANES] for n in range(lines)]
            + [jnp.zeros((8 - lines, LANES), F32)],
            axis=0,
        )
    )
    norm_copies = [send(norm_lane.at[0], norm_lane.at[s], z_peer(s)) for s in FAR_Z]
    bias = jnp.concatenate(
        [ebias_ref[pl.ds(r * lines + n, 1), :] for n in range(lines)], axis=1
    )

    def encode(h):
        arrived(encoded[h])
        value = keep[h, span(z * piece, piece)] + bias
        for n in range(3, 7):
            value = value + rs_wide[h, n]
        pre[h] = value
        lat[own_piece(h)] = jnp.maximum(value, 0.0).astype(BF16)
        return z_gather(lat, h)

    gathers = [encode(h) for h in range(2)]

    def block(buf, h, place):
        return buf.at[h, lax.rem(place, 2), span(lax.div(place, 2) * part, part)]

    place = x * SIDE + y
    feature = lax.rem(place, 2)

    def rebuild(h):
        arrived(gathers[h])
        acts = lat[side_rows(h, c)]
        for f in range(2):
            product = dot_nn(acts, dec[f])
            rb[h, f] = product
            rb_low[h, f] = product.astype(BF16)
        copies = []
        for dx, dy in FAR_XY:
            px, py = at_xy(dx, dy)
            piece_low = block(rb_low, h, px * SIDE + py)
            copies.append(
                send(piece_low, rs_xy.at[h, dx * SIDE + dy], xy_peer(dx, dy))
            )
        return copies

    scatters = [rebuild(h) for h in range(2)]
    lat_copies = [
        send(lat.at[side_rows(h, c)], lat.at[side_rows(h, c)], pair) for h in range(2)
    ]

    def residual(h):
        arrived(scatters[h])
        total = block(rb, h, place)[...]
        for n in range(1, SIDE * SIDE):
            total = total + rs_xy[h, n].astype(F32)
        from_rows = span(h * rows + c * side + lax.div(place, 2) * part, part)
        acts = tok[feature, from_rows].astype(F32)
        grad_rows = 2.0 * (total + dbias[feature] - acts) / total_rows
        ref = block(gside, h, place)
        ref[...] = grad_rows.astype(BF16)
        return [send(ref, ref, xy_peer(*s)) for s in FAR_XY]

    gathers = [residual(h) for h in range(2)]
    arrived(norm_copies)
    strength = norm_lane[0]
    for s in range(1, CHIPS):
        strength = strength + norm_lane[s]
    strength = row_scale * strength
    penalty = jnp.concatenate([strength[n : n + 1, :] for n in range(lines)], axis=1)
    def back_start(h):
        arrived(gathers[h])
        total = dot_nt(gside[h, 0], dec[0]) + dot_nt(gside[h, 1], dec[1])
        keep[2 + h] = total
        half[h] = total.astype(BF16)
        return z_scatter(half.at[h], rs_z.at[h])

    scatters = [back_start(h) for h in range(2)]

    grad_copies = [
        send(gside.at[h, 1], grad.at[side_rows(h, c)], pair) for h in range(2)
    ]
    for h in range(2):
        grad[side_rows(h, c)] = gside[h, 0]
    arrived([acts_back])
    tok_out[...] = tok[0]
    for load in loads[3:8]:
        load.wait()
    arrived(lat_copies)
    arrived(grad_copies)
    ones_rows = jnp.ones((total_rows, LANES), BF16)

    def decoder_block(n, carry):
        at = span(n * LANES, LANES)
        acts = lat[:, at]
        gradient = dot_tn(acts, grad[...])
        factor = row_scale * dot_tn(acts, ones_rows) / norm_col[at]
        weight = dec[0, at]
        gradient = gradient + jnp.tile(factor, (1, width // LANES)) * weight.astype(F32)
        w_new[at], m_new[at], v_new[at] = adam_step(weight, m_old[at], v_old[at], gradient)
        return carry

    def back(h):
        arrived(scatters[h])
        value = keep[2 + h, span(z * piece, piece)] + penalty
        for s in range(1, CHIPS):
            value = value + rs_z[h, s].astype(F32)
        gpre[own_piece(h)] = jnp.where(pre[h] > 0, value, 0.0).astype(BF16)
        return z_gather(gpre, h)

    def forward(h):
        arrived(gathers[h])
        ref = gpre.at[side_rows(h, c)]
        return send(ref, ref, pair)

    lax.fori_loop(0, EARLY, decoder_block, 0)
    gathers = [back(h) for h in range(2)]
    lax.fori_loop(EARLY, LATE, decoder_block, 0)
    last = [forward(0)]
    lax.fori_loop(LATE, lines, decoder_block, 0)
    last.append(forward(1))
    row_sum = dot_nn(jnp.ones((8, total_rows), BF16), grad[...])
    rsum_out[...] = jnp.concatenate(
        [row_sum[0:1, n * LANES : (n + 1) * LANES] for n in range(width // LANES)], axis=0
    )
    for h in range(2):
        gpre_out[side_rows(h, c)] = gpre[side_rows(h, c)]
    for copy in sent:
        copy.wait_send()
    for h in range(2):
        arrived(last[h : h + 1])
        gpre_out[side_rows(h, 1 - c)] = gpre[side_rows(h, 1 - c)]
    assert count[0] == SENDS


def exchange(acts, enc_weight, dec_weight, dec_m, dec_v, enc_m, enc_v, enc_bias, dec_bias):
    rows, width = acts.shape
    latents = enc_weight.shape[1]
    total_rows = 2 * rows
    side = rows // 2
    piece = side // CHIPS
    part = 2 * side // (SIDE * SIDE)
    hbm = pl.BlockSpec(memory_space=pltpu.HBM)
    vmem = pl.BlockSpec(memory_space=pltpu.VMEM)
    dec_shape = (latents, width)
    return pl.pallas_call(
        exchange_kernel,
        name="exchange",
        out_shape=(
            jax.ShapeDtypeStruct((total_rows, width), BF16),
            jax.ShapeDtypeStruct((total_rows, latents), BF16),
            *[jax.ShapeDtypeStruct(dec_shape, BF16)] * 3,
            *[jax.ShapeDtypeStruct(enc_weight.shape, BF16)] * 3,
            jax.ShapeDtypeStruct((width // LANES, LANES), F32),
        ),
        in_specs=[hbm] * 9,
        out_specs=(vmem,) * 9,
        scratch_shapes=[
            pltpu.VMEM((2, total_rows, width), BF16),
            pltpu.VMEM((2, width, latents), BF16),
            pltpu.VMEM((2, *dec_shape), BF16),
            pltpu.VMEM((2, 1, width), F32),
            pltpu.VMEM((total_rows, latents), BF16),
            pltpu.VMEM((2, 2, side, width), BF16),
            pltpu.VMEM((total_rows, width), BF16),
            pltpu.VMEM((total_rows, latents), BF16),
            pltpu.VMEM((4, side, latents), F32),
            pltpu.VMEM((2, side, latents), BF16),
            pltpu.VMEM((2, 7, piece, latents), F32),
            pltpu.VMEM((2, 2, piece, latents), F32),
            pltpu.VMEM((2, CHIPS, piece, latents), BF16),
            pltpu.VMEM((2, piece, latents), F32),
            pltpu.VMEM((2, 2, side, width), F32),
            pltpu.VMEM((2, 2, side, width), BF16),
            pltpu.VMEM((2, SIDE * SIDE, part, width), BF16),
            pltpu.VMEM((CHIPS, 8, LANES), F32),
            pltpu.VMEM((latents, LANES), F32),
            *[pltpu.VMEM(dec_shape, BF16)] * 2,
            pltpu.VMEM(enc_bias.shape, F32),
            pltpu.VMEM(dec_bias.shape, F32),
            pltpu.SemaphoreType.DMA((10,)),
            pltpu.SemaphoreType.DMA((SENDS,)),
            pltpu.SemaphoreType.DMA((SENDS,)),
        ],
        compiler_params=pltpu.CompilerParams(
            collective_id=0, has_side_effects=True, vmem_limit_bytes=30 << 20
        ),
    )(acts, enc_weight, dec_weight, dec_m, dec_v, enc_m, enc_v, enc_bias, dec_bias)


def finish_kernel(
    tok_ref, gpre_ref, w_done, m_done, v_done, w, m, v, rsum_ref,
    w_next, m_next, v_next, bsum_out, rsum_out, w_out, m_out, v_out, sem,
):
    blocks = pl.num_programs(0)
    step = pl.program_id(0)
    copies = [
        pltpu.make_async_copy(src, dst, sem.at[n])
        for n, (src, dst) in enumerate(((w_done, w_out), (m_done, m_out), (v_done, v_out)))
    ]

    @pl.when(step == 0)
    def _():
        for copy in copies:
            copy.start()
        total = dot_nn(jnp.ones((8, gpre_ref.shape[0]), BF16), gpre_ref[...])
        for n in range(bsum_out.shape[0]):
            bsum_out[n : n + 1, :] = total[0:1, n * LANES : (n + 1) * LANES]
        rsum_out[...] = rsum_ref[...]

    size = w_next.shape[0]
    at = pl.ds(pl.multiple_of(step * size, size), size)
    gradient = dot_tn(tok_ref[:, at], gpre_ref[...])
    w_next[...], m_next[...], v_next[...] = adam_step(w[at], m[at], v[at], gradient)

    @pl.when(step == blocks - 1)
    def _():
        for copy in copies:
            copy.wait()


def finish(tok, gpre, decoder, encoder, row_sum, blocks=2):
    latents, width = decoder[0].shape
    block = pl.BlockSpec((width // blocks, latents), lambda i: (i, 0))
    vmem = pl.BlockSpec(memory_space=pltpu.VMEM)
    hbm = pl.BlockSpec(memory_space=pltpu.HBM)

    def whole(shape):
        return pl.BlockSpec(shape, lambda i: (0, 0))

    shapes = (latents // LANES, LANES), (width // LANES, LANES)
    return pl.pallas_call(
        finish_kernel,
        name="finish",
        grid=(blocks,),
        out_shape=(jax.ShapeDtypeStruct((width, latents), BF16),) * 3
        + tuple(jax.ShapeDtypeStruct(s, F32) for s in shapes)
        + (jax.ShapeDtypeStruct((latents, width), BF16),) * 3,
        in_specs=[vmem] * 9,
        out_specs=(block,) * 3 + tuple(whole(s) for s in shapes) + (hbm,) * 3,
        scratch_shapes=[pltpu.SemaphoreType.DMA((3,))],
        compiler_params=pltpu.CompilerParams(vmem_limit_bytes=40 << 20),
    )(tok, gpre, *decoder, *encoder, row_sum)


def local(
    model_acts, enc_weight, dec_weight, enc_bias, dec_bias,
    enc_first, enc_second, dec_first, dec_second,
):
    moments = dec_first, dec_second, enc_first, enc_second
    biases = enc_bias.reshape(-1, LANES), dec_bias.reshape(-1, LANES)
    results = exchange(
        *(
            pltpu.with_memory_space_constraint(a, pltpu.HBM)
            for a in (model_acts, enc_weight, dec_weight, *moments, *biases)
        )
    )
    tok, gpre, row_sum = results[0], results[1], results[8]
    enc_next, enc_m, enc_v, bias_sum, row_sum, dec_next, dec_m, dec_v = finish(
        tok, gpre, results[2:5], results[5:8], row_sum
    )
    return (
        enc_next, dec_next, enc_m, enc_v, dec_m, dec_v,
        bias_sum.reshape(-1), row_sum.reshape(-1),
    )


def solution(mesh):
    split = P("expert", ("latent", "row"))
    turned = P(("latent", "row"), "expert")
    return jax.shard_map(
        local,
        mesh=mesh,
        in_specs=(
            P("row", "expert"), split, turned, P("latent"), P("expert"),
            split, split, turned, turned,
        ),
        out_specs=(
            split, turned, split, split, turned, turned,
            P(("latent", "row")), P("expert"),
        ),
        check_vma=False,
    )
```

```python
import functools

import jax
import jax.numpy as jnp
from jax import lax
from jax.experimental import pallas as pl
from jax.experimental.pallas import tpu as pltpu
from jax.sharding import PartitionSpec as P

beta_one = 0.9
beta_two = 0.999
learn_rate = 0.001
adam_eps = 1e-08
bias_one = 0.9999734386011124
bias_two = 0.09520785288629115
norm_eps = 1e-06
sparsity = 1.0

MESH = pl.DeviceIdType.MESH
F32 = jnp.float32
BF16 = jnp.bfloat16

CHIPS = 8
SIDE = 4
LANES = 128
ORIENT = (1, -1)
SENDS = 136
EARLY, LATE = 2, 5
FAR_Z = (4, 3, 5, 2, 6, 1, 7)
FAR_XY = tuple(
    sorted(
        ((a, b) for a in range(SIDE) for b in range(SIDE) if a or b),
        key=lambda s: -(min(s[0], SIDE - s[0]) + min(s[1], SIDE - s[1])),
    )
)


def dot_nt(left, right):
    return lax.dot_general(
        left, right, (((1,), (1,)), ((), ())), preferred_element_type=F32
    )


def dot_tn(left, right):
    return lax.dot_general(
        left, right, (((0,), (0,)), ((), ())), preferred_element_type=F32
    )


def dot_nn(left, right):
    return jnp.dot(left, right, preferred_element_type=F32)


def adam_step(weight, moment_one, moment_two, gradient):
    first_next = beta_one * moment_one.astype(F32) + (1.0 - beta_one) * gradient
    second_next = beta_two * moment_two.astype(F32) + (1.0 - beta_two) * (gradient * gradient)
    root = bias_two**0.5
    move = (learn_rate * root / bias_one) * first_next / (jnp.sqrt(second_next) + adam_eps * root)
    stepped = weight.astype(F32) - move
    return stepped.astype(BF16), first_next.astype(BF16), second_next.astype(BF16)


def exchange_kernel(
    acts_hbm, enc_hbm, dec_hbm, dec_m_hbm, dec_v_hbm, enc_m_hbm, enc_v_hbm,
    ebias_hbm, dbias_hbm,
    tok_out, gpre_out, w_new, m_new, v_new, enc_out, enc_m_out, enc_v_out, rsum_out,
    tok, enc, dec, dbias, lat, gside, grad, gpre,
    keep, half, rs_wide, relay, rs_z, pre,
    rb, rb_low, rs_xy, norm_lane, norm_col,
    m_old, v_old, ebias_ref, dbias_ref, load_sem, send_sem, recv_sem,
):
    rows, width = acts_hbm.shape
    latents = enc_hbm.shape[1]
    total_rows = 2 * rows
    side = rows // 2
    piece = side // CHIPS
    lines = latents // LANES
    part = 2 * side // (SIDE * SIDE)
    row_scale = sparsity / total_rows

    e, l, r = (lax.axis_index(a) for a in ("expert", "latent", "row"))
    z, c = lax.div(e, 2), lax.rem(e, 2)
    y, x = lax.div(l, 2), 2 * r + lax.rem(l, 2)

    def at_z(step):
        return lax.rem(z + step + CHIPS, CHIPS)

    def z_peer(step):
        return (at_z(step) * 2 + c, l, r)

    def at_xy(dx, dy):
        return lax.rem(x + dx, SIDE), lax.rem(y + dy, SIDE)

    def xy_peer(dx, dy):
        px, py = at_xy(dx, dy)
        return (e, py * 2 + lax.rem(px, 2), lax.div(px, 2))

    mirror_x = SIDE - 1 - x
    mirror_l, mirror_r = y * 2 + lax.rem(mirror_x, 2), lax.div(mirror_x, 2)
    other = z * 2 + 1 - c
    pair = (other, l, r)
    mirror, mirror_pair = (e, mirror_l, mirror_r), (other, mirror_l, mirror_r)

    count = [0]
    sent = []

    def send(src, dst, to):
        n = count[0]
        count[0] += 1
        copy = pltpu.make_async_remote_copy(
            src_ref=src, dst_ref=dst, send_sem=send_sem.at[n], recv_sem=recv_sem.at[n],
            device_id=to, device_id_type=MESH,
        )
        copy.start()
        sent.append(copy)
        return copy

    def arrived(copies):
        for copy in copies:
            copy.wait_recv()

    def span(start, size):
        return pl.ds(pl.multiple_of(start, size), size)

    def side_rows(h, core):
        return span(h * rows + core * side, side)

    def own_piece(h):
        return span(h * rows + c * side + z * piece, piece)

    loads = [
        pltpu.make_async_copy(src, dst, load_sem.at[n])
        for n, (src, dst) in enumerate(
            (
                (acts_hbm, tok.at[0, span(r * rows, rows)]),
                (enc_hbm, enc.at[0]), (dec_hbm, dec.at[0]),
                (dec_m_hbm, m_old), (dec_v_hbm, v_old), (enc_hbm, enc_out),
                (enc_m_hbm, enc_m_out), (enc_v_hbm, enc_v_out), (ebias_hbm, ebias_ref),
                (dbias_hbm, dbias_ref),
            )
        )
    ]
    barrier = pltpu.get_barrier_semaphore()
    greeted = [
        *(z_peer(s) for s in FAR_Z), *(xy_peer(*s) for s in FAR_XY), mirror_pair, pair
    ]
    for to in greeted:
        pl.semaphore_signal(barrier, inc=1, device_id=to, device_id_type=MESH)
    for load in loads[:3] + loads[8:]:
        load.start()
    pl.semaphore_wait(barrier, len(greeted))

    give = side_rows(r, 1 - c)
    give_hbm = acts_hbm.at[span((1 - c) * side, side)]
    acts_far = [
        send(acts_hbm.at[span(c * side, side)], tok.at[0, side_rows(r, c)], mirror),
        send(give_hbm, tok.at[1, give], mirror_pair),
    ]
    acts_pair = send(give_hbm, tok.at[1, give], pair)
    enc_pair = send(enc_hbm, enc.at[1], pair)
    dec_pair = send(dec_hbm, dec.at[1], pair)
    for load in loads[3:8]:
        load.start()
    for load in loads[8:]:
        load.wait()
    dbias[0] = jnp.concatenate(
        [dbias_ref[n : n + 1, :] for n in range(width // LANES)], axis=1
    )
    for load in loads[:2]:
        load.wait()

    ones_lane = jnp.ones((8, width), BF16)
    ones_col = jnp.ones((width, LANES), BF16)

    def squares(f):
        wide = dec[f].astype(F32)
        square = wide * wide
        high = square.astype(BF16)
        low = (square - high.astype(F32)).astype(BF16)
        return (
            dot_nt(ones_lane, high) + dot_nt(ones_lane, low),
            dot_nn(high, ones_col) + dot_nn(low, ones_col),
        )

    def z_part(values, step):
        return values.at[span(at_z(step) * piece, piece)]

    def z_scatter(values, slots):
        return [send(z_part(values, s), slots.at[s], z_peer(s)) for s in FAR_Z]

    def relay_start(values, slots, s):
        return [
            send(z_part(values, n), slots.at[i], z_peer(to))
            for i, (n, to) in enumerate(
                ((4 * s, -2 * s), (-3 * s, -s), (3 * s, s), (-s, -s), (s, s))
            )
        ]

    def relay_pass(values, slots, hold, copies, s):
        arrived(copies[:2])
        hold[0] = z_part(values, -2 * s)[...] + slots[0] + slots[1]
        back = send(hold.at[0], slots.at[5], z_peer(-2 * s))
        arrived(copies[2:3])
        hold[1] = z_part(values, 2 * s)[...] + slots[2]
        return [*copies[3:], back, send(hold.at[1], slots.at[6], z_peer(2 * s))]

    def z_gather(buf, h):
        at = own_piece(h)
        return [send(buf.at[at], buf.at[at], z_peer(s)) for s in FAR_Z]

    def near_gather(buf, h, s):
        at = own_piece(h)
        return [send(buf.at[at], buf.at[at], z_peer(n)) for n in (2 * s, -2 * s, -s, s)]

    def far_gather(buf, h, copies, s):
        def piece_of(step):
            return buf.at[span(h * rows + c * side + at_z(step) * piece, piece)]

        arrived(copies[1:2])
        far = [send(piece_of(2 * s), piece_of(2 * s), z_peer(n * s)) for n in (-2, -1)]
        arrived(copies[:1])
        far.append(send(piece_of(-2 * s), piece_of(-2 * s), z_peer(s)))
        return copies[2:] + far

    loads[2].wait()
    lane, column = squares(0)
    arrived([dec_pair])
    more_lane, more_column = squares(1)
    norm_col[...] = jnp.sqrt(column + more_column + norm_eps)
    lane = jnp.sqrt(lane + more_lane + norm_eps)
    norm_lane[0] = jnp.concatenate(
        [lane[0:1, n * LANES : (n + 1) * LANES] for n in range(lines)]
        + [jnp.zeros((8 - lines, LANES), F32)],
        axis=0,
    )
    arrived([acts_pair, enc_pair, *acts_far])
    encoded = []
    for h, s in enumerate((1, -1)):
        at = side_rows(h, c)
        keep[h] = dot_nn(tok[0, at], enc[0]) + dot_nn(tok[1, at], enc[1])
        encoded.append(relay_start(keep.at[h], rs_wide.at[h], s))
    bias_pair = send(dbias.at[0], dbias.at[1], pair)
    theirs = side_rows(1 - r, c)
    acts_back = send(tok.at[1, theirs], tok.at[0, theirs], pair)
    for h, s in enumerate((1, -1)):
        encoded[h] = relay_pass(keep.at[h], rs_wide.at[h], relay.at[h], encoded[h], s)

    norm_copies = [send(norm_lane.at[0], norm_lane.at[s], z_peer(s)) for s in FAR_Z]
    arrived([bias_pair])
    bias = jnp.concatenate(
        [ebias_ref[pl.ds(r * lines + n, 1), :] for n in range(lines)], axis=1
    )

    def encode(h):
        arrived(encoded[h])
        value = keep[h, span(z * piece, piece)] + bias
        for n in range(3, 7):
            value = value + rs_wide[h, n]
        pre[h] = value
        lat[own_piece(h)] = jnp.maximum(value, 0.0).astype(BF16)
        return z_gather(lat, h)

    gathers = [encode(h) for h in range(2)]

    def block(buf, h, place):
        return buf.at[h, lax.rem(place, 2), span(lax.div(place, 2) * part, part)]

    place = x * SIDE + y
    feature = lax.rem(place, 2)

    def rebuild(h):
        arrived(gathers[h])
        acts = lat[side_rows(h, c)]
        for f in range(2):
            product = dot_nn(acts, dec[f])
            rb[h, f] = product
            rb_low[h, f] = product.astype(BF16)
        copies = []
        for dx, dy in FAR_XY:
            px, py = at_xy(dx, dy)
            piece_low = block(rb_low, h, px * SIDE + py)
            copies.append(
                send(piece_low, rs_xy.at[h, dx * SIDE + dy], xy_peer(dx, dy))
            )
        return copies

    scatters = [rebuild(h) for h in range(2)]
    lat_copies = [
        send(lat.at[side_rows(h, c)], lat.at[side_rows(h, c)], pair) for h in range(2)
    ]

    def residual(h):
        arrived(scatters[h])
        total = block(rb, h, place)[...]
        for n in range(1, SIDE * SIDE):
            total = total + rs_xy[h, n].astype(F32)
        from_rows = span(h * rows + c * side + lax.div(place, 2) * part, part)
        acts = tok[feature, from_rows].astype(F32)
        grad_rows = 2.0 * (total + dbias[feature] - acts) / total_rows
        ref = block(gside, h, place)
        ref[...] = grad_rows.astype(BF16)
        return [send(ref, ref, xy_peer(*s)) for s in FAR_XY]

    gathers = [residual(h) for h in range(2)]
    arrived(norm_copies)
    strength = norm_lane[0]
    for s in range(1, CHIPS):
        strength = strength + norm_lane[s]
    strength = row_scale * strength
    penalty = jnp.concatenate([strength[n : n + 1, :] for n in range(lines)], axis=1)
    def back_start(h):
        arrived(gathers[h])
        total = dot_nt(gside[h, 0], dec[0]) + dot_nt(gside[h, 1], dec[1])
        keep[2 + h] = total
        half[h] = total.astype(BF16)
        return z_scatter(half.at[h], rs_z.at[h])

    scatters = [back_start(h) for h in range(2)]

    grad_copies = [
        send(gside.at[h, 1], grad.at[side_rows(h, c)], pair) for h in range(2)
    ]
    for h in range(2):
        grad[side_rows(h, c)] = gside[h, 0]
    arrived([acts_back])
    tok_out[...] = tok[0]
    for load in loads[3:8]:
        load.wait()
    arrived(lat_copies)
    arrived(grad_copies)
    ones_rows = jnp.ones((total_rows, LANES), BF16)

    def decoder_block(n, carry):
        at = span(n * LANES, LANES)
        acts = lat[:, at]
        gradient = dot_tn(acts, grad[...])
        factor = row_scale * dot_tn(acts, ones_rows) / norm_col[at]
        weight = dec[0, at]
        gradient = gradient + jnp.tile(factor, (1, width // LANES)) * weight.astype(F32)
        w_new[at], m_new[at], v_new[at] = adam_step(weight, m_old[at], v_old[at], gradient)
        return carry

    def back(h):
        arrived(scatters[h])
        value = keep[2 + h, span(z * piece, piece)] + penalty
        for s in range(1, CHIPS):
            value = value + rs_z[h, s].astype(F32)
        gpre[own_piece(h)] = jnp.where(pre[h] > 0, value, 0.0).astype(BF16)
        return near_gather(gpre, h, ORIENT[h])

    def forward(h):
        arrived(gathers[h])
        ref = gpre.at[side_rows(h, c)]
        return send(ref, ref, pair)

    lax.fori_loop(0, EARLY, decoder_block, 0)
    gathers = [back(h) for h in range(2)]
    gathers = [far_gather(gpre, h, gathers[h], ORIENT[h]) for h in range(2)]
    lax.fori_loop(EARLY, LATE, decoder_block, 0)
    last = [forward(0)]
    lax.fori_loop(LATE, lines, decoder_block, 0)
    last.append(forward(1))
    row_sum = dot_nn(jnp.ones((8, total_rows), BF16), grad[...])
    rsum_out[...] = jnp.concatenate(
        [row_sum[0:1, n * LANES : (n + 1) * LANES] for n in range(width // LANES)], axis=0
    )
    for h in range(2):
        gpre_out[side_rows(h, c)] = gpre[side_rows(h, c)]
    for copy in sent:
        copy.wait_send()
    for h in range(2):
        arrived(last[h : h + 1])
        gpre_out[side_rows(h, 1 - c)] = gpre[side_rows(h, 1 - c)]
    assert count[0] == SENDS


def exchange(acts, enc_weight, dec_weight, dec_m, dec_v, enc_m, enc_v, enc_bias, dec_bias):
    rows, width = acts.shape
    latents = enc_weight.shape[1]
    total_rows = 2 * rows
    side = rows // 2
    piece = side // CHIPS
    part = 2 * side // (SIDE * SIDE)
    hbm = pl.BlockSpec(memory_space=pltpu.HBM)
    vmem = pl.BlockSpec(memory_space=pltpu.VMEM)
    dec_shape = (latents, width)
    return pl.pallas_call(
        exchange_kernel,
        name="exchange",
        out_shape=(
            jax.ShapeDtypeStruct((total_rows, width), BF16),
            jax.ShapeDtypeStruct((total_rows, latents), BF16),
            *[jax.ShapeDtypeStruct(dec_shape, BF16)] * 3,
            *[jax.ShapeDtypeStruct(enc_weight.shape, BF16)] * 3,
            jax.ShapeDtypeStruct((width // LANES, LANES), F32),
        ),
        in_specs=[hbm] * 9,
        out_specs=(vmem,) * 9,
        scratch_shapes=[
            pltpu.VMEM((2, total_rows, width), BF16),
            pltpu.VMEM((2, width, latents), BF16),
            pltpu.VMEM((2, *dec_shape), BF16),
            pltpu.VMEM((2, 1, width), F32),
            pltpu.VMEM((total_rows, latents), BF16),
            pltpu.VMEM((2, 2, side, width), BF16),
            pltpu.VMEM((total_rows, width), BF16),
            pltpu.VMEM((total_rows, latents), BF16),
            pltpu.VMEM((4, side, latents), F32),
            pltpu.VMEM((2, side, latents), BF16),
            pltpu.VMEM((2, 7, piece, latents), F32),
            pltpu.VMEM((2, 2, piece, latents), F32),
            pltpu.VMEM((2, CHIPS, piece, latents), BF16),
            pltpu.VMEM((2, piece, latents), F32),
            pltpu.VMEM((2, 2, side, width), F32),
            pltpu.VMEM((2, 2, side, width), BF16),
            pltpu.VMEM((2, SIDE * SIDE, part, width), BF16),
            pltpu.VMEM((CHIPS, 8, LANES), F32),
            pltpu.VMEM((latents, LANES), F32),
            *[pltpu.VMEM(dec_shape, BF16)] * 2,
            pltpu.VMEM(enc_bias.shape, F32),
            pltpu.VMEM(dec_bias.shape, F32),
            pltpu.SemaphoreType.DMA((10,)),
            pltpu.SemaphoreType.DMA((SENDS,)),
            pltpu.SemaphoreType.DMA((SENDS,)),
        ],
        compiler_params=pltpu.CompilerParams(
            collective_id=0, has_side_effects=True, vmem_limit_bytes=30 << 20
        ),
    )(acts, enc_weight, dec_weight, dec_m, dec_v, enc_m, enc_v, enc_bias, dec_bias)


def finish_kernel(
    tok_ref, gpre_ref, w_done, m_done, v_done, w, m, v, rsum_ref,
    w_next, m_next, v_next, bsum_out, rsum_out, w_out, m_out, v_out, sem,
):
    blocks = pl.num_programs(0)
    step = pl.program_id(0)
    copies = [
        pltpu.make_async_copy(src, dst, sem.at[n])
        for n, (src, dst) in enumerate(((w_done, w_out), (m_done, m_out), (v_done, v_out)))
    ]

    @pl.when(step == 0)
    def _():
        for copy in copies:
            copy.start()
        total = dot_nn(jnp.ones((8, gpre_ref.shape[0]), BF16), gpre_ref[...])
        for n in range(bsum_out.shape[0]):
            bsum_out[n : n + 1, :] = total[0:1, n * LANES : (n + 1) * LANES]
        rsum_out[...] = rsum_ref[...]

    size = w_next.shape[0]
    at = pl.ds(pl.multiple_of(step * size, size), size)
    gradient = dot_tn(tok_ref[:, at], gpre_ref[...])
    w_next[...], m_next[...], v_next[...] = adam_step(w[at], m[at], v[at], gradient)

    @pl.when(step == blocks - 1)
    def _():
        for copy in copies:
            copy.wait()


def finish(tok, gpre, decoder, encoder, row_sum, blocks=2):
    latents, width = decoder[0].shape
    block = pl.BlockSpec((width // blocks, latents), lambda i: (i, 0))
    vmem = pl.BlockSpec(memory_space=pltpu.VMEM)
    hbm = pl.BlockSpec(memory_space=pltpu.HBM)

    def whole(shape):
        return pl.BlockSpec(shape, lambda i: (0, 0))

    shapes = (latents // LANES, LANES), (width // LANES, LANES)
    return pl.pallas_call(
        finish_kernel,
        name="finish",
        grid=(blocks,),
        out_shape=(jax.ShapeDtypeStruct((width, latents), BF16),) * 3
        + tuple(jax.ShapeDtypeStruct(s, F32) for s in shapes)
        + (jax.ShapeDtypeStruct((latents, width), BF16),) * 3,
        in_specs=[vmem] * 9,
        out_specs=(block,) * 3 + tuple(whole(s) for s in shapes) + (hbm,) * 3,
        scratch_shapes=[pltpu.SemaphoreType.DMA((3,))],
        compiler_params=pltpu.CompilerParams(vmem_limit_bytes=40 << 20),
    )(tok, gpre, *decoder, *encoder, row_sum)


def local(
    model_acts, enc_weight, dec_weight, enc_bias, dec_bias,
    enc_first, enc_second, dec_first, dec_second,
):
    moments = dec_first, dec_second, enc_first, enc_second
    biases = enc_bias.reshape(-1, LANES), dec_bias.reshape(-1, LANES)
    results = exchange(
        *(
            pltpu.with_memory_space_constraint(a, pltpu.HBM)
            for a in (model_acts, enc_weight, dec_weight, *moments, *biases)
        )
    )
    tok, gpre, row_sum = results[0], results[1], results[8]
    enc_next, enc_m, enc_v, bias_sum, row_sum, dec_next, dec_m, dec_v = finish(
        tok, gpre, results[2:5], results[5:8], row_sum
    )
    return (
        enc_next, dec_next, enc_m, enc_v, dec_m, dec_v,
        bias_sum.reshape(-1), row_sum.reshape(-1),
    )


def solution(mesh):
    split = P("expert", ("latent", "row"))
    turned = P(("latent", "row"), "expert")
    return jax.shard_map(
        local,
        mesh=mesh,
        in_specs=(
            P("row", "expert"), split, turned, P("latent"), P("expert"),
            split, split, turned, turned,
        ),
        out_specs=(
            split, turned, split, split, turned, turned,
            P(("latent", "row")), P("expert"),
        ),
        check_vma=False,
    )
```
